128 devices in a mesh: slab: 16 (over x, z), energy: 8 (over y, core).
Axes of the slice: x: 4, y: 4, z: 4, core: 2. Of those that a mesh axis runs over, the one named last changes fastest.
Arguments:
- green_lesser: bfloat16 [2, 16, 64, 256, 256], P(None, 'energy', 'slab'), may hold values from -4 to 4
- screened_lesser: bfloat16 [2, 16, 64, 256, 256], P(None, 'energy', 'slab'), may hold values from -4 to 4
- green_retarded: bfloat16 [2, 16, 64, 256, 256], P(None, 'energy', 'slab'), may hold values from -1 to 1
- coupling: bfloat16 [2, 64, 256, 256], P(None, 'slab'), may hold values from -1 to 1
Outputs:
- connected_lesser: float32 [2, 16, 64, 256, 256], P(None, 'energy', 'slab')
The draws below stay inside these ranges and needn't reach their ends.
All inputs are finite; a program needn't handle non-finite values.
Results may differ from the reference program's by a relative error of at most 0.004.
Values may be sent and summed in bfloat16 or wider, within the bound.
A program may use at most 128 MiB of HBM per device.

```python
import math
import jax
import jax.numpy as jnp
from jax import lax

NORB = 256
SLABS = 64
ENERGIES = 16


def shuffled(single):
    return jax.random.permutation(single, NORB)


def unitary_blocks(key, leading, factor, noise_level):
    blocks_total = math.prod(leading)
    subkeys = jax.random.split(key, 5)
    row_order = jax.vmap(shuffled)(jax.random.split(subkeys[0], blocks_total)).astype(jnp.int32)
    column_order = jax.vmap(shuffled)(jax.random.split(subkeys[1], blocks_total)).astype(jnp.int32)
    row_phase = jax.random.uniform(subkeys[2], (blocks_total, NORB), jnp.float32, -math.pi, math.pi)
    column_phase = jax.random.uniform(subkeys[3], (blocks_total, NORB), jnp.float32, -math.pi, math.pi)
    product_index = row_order[:, :, None] * column_order[:, None, :] % NORB
    angles = row_phase[:, :, None] + column_phase[:, None, :] + 2.0 * math.pi / NORB * product_index.astype(jnp.float32)
    spread = noise_level / math.sqrt(2.0 * NORB)
    full_shape = (2, blocks_total, NORB, NORB)
    disorder = jax.random.truncated_normal(subkeys[4], -4.0, 4.0, full_shape, jnp.float32) * spread
    unitary_part = jnp.stack([jnp.cos(angles), jnp.sin(angles)]) / math.sqrt(NORB)
    result = factor * (unitary_part + disorder)
    return result.reshape((2,) + tuple(leading) + (NORB, NORB))


def draw_green_retarded(key, part):
    return unitary_blocks(jax.random.fold_in(key, 101), (ENERGIES, SLABS), 0.98, 0.2).astype(jnp.bfloat16)


def draw_coupling(key, part):
    return unitary_blocks(jax.random.fold_in(key, 202), (SLABS,), 0.975, 0.2).astype(jnp.bfloat16)


def shard_levels(key, extent, pieces, low, top_value):
    gain, own = 1.0, jax.random.fold_in(key, 6)
    for dim, shards_of in pieces:
        steps = jnp.exp(jax.random.uniform(jax.random.fold_in(own, dim), (shards_of,), jnp.float32, low / len(pieces), top_value / len(pieces)))
        gain = gain * jnp.repeat(steps, extent[dim] // shards_of).reshape([-1 if axis == dim else 1 for axis in range(len(extent))])
    return gain


def noise(stream_key, shape, scale, reach, cuts=(), held_as=jnp.bfloat16):
    values = jax.random.normal(stream_key, shape, jnp.float32) * scale
    if len(cuts) > 0:
        values = shard_levels(stream_key, shape, cuts, -0.22, 0.18) * values
    return jnp.clip(values, min=-reach, max=reach).astype(held_as)


def setup_inputs(seed: int = 0) -> dict:
    keys = jax.random.split(jax.random.key(seed), 5)
    green_lesser = noise(keys[0], (2, ENERGIES, SLABS, NORB, NORB), 1.0, 4.0, ((1, 8), (2, 16)))
    screened_lesser = noise(keys[1], (2, ENERGIES, SLABS, NORB, NORB), 1.0, 4.0, ((1, 8), (2, 16)))
    green_retarded = draw_green_retarded(jax.random.fold_in(keys[4], 71), 0)
    coupling = draw_coupling(jax.random.fold_in(keys[4], 71), 0)
    return {"green_lesser": green_lesser, "screened_lesser": screened_lesser, "green_retarded": green_retarded, "coupling": coupling}


def convolve_energy(green, screen):
    points = green.shape[1]
    middle = points // 2
    widths = [(0, 0)] * green.ndim
    widths[1] = (points, points)
    padded = jnp.pad(green.astype(jnp.float32), widths)
    screen_wide = screen.astype(jnp.float32)

    def add_offset(offset, totals):
        start = (points + middle - offset).astype(jnp.int32)
        shifted = lax.dynamic_slice_in_dim(padded, start, points, 1)
        weight = lax.dynamic_slice_in_dim(screen_wide, offset.astype(jnp.int32), 1, 1)
        real_part = totals[0] + shifted[0] * weight[0] - shifted[1] * weight[1]
        imag_part = totals[1] + shifted[0] * weight[1] + shifted[1] * weight[0]
        return (real_part, imag_part)

    blank_sum = jnp.zeros(green.shape[1:], jnp.float32)
    totals = lax.fori_loop(0, points, add_offset, (blank_sum, blank_sum))
    return jnp.stack([-totals[1] / points, totals[0] / points]).astype(jnp.bfloat16)


def precise(first, second):
    return jnp.dot(first, second, precision=lax.Precision.HIGHEST, preferred_element_type=jnp.float32)


def lowdot(first, second):
    return jnp.dot(first, second, preferred_element_type=jnp.float32)


def congruence(kernel, state, source):
    inner_re = precise(kernel[0], state[0]) - precise(kernel[1], state[1])
    inner_im = precise(kernel[0], state[1]) + precise(kernel[1], state[0])
    outer_re = precise(inner_re, kernel[0].T) + precise(inner_im, kernel[1].T)
    outer_im = precise(inner_im, kernel[0].T) - precise(inner_re, kernel[1].T)
    return (outer_re + source[0], outer_im + source[1])


def reference(green_lesser, screened_lesser, green_retarded, coupling):
    lesser_slabs = jnp.moveaxis(green_lesser, 2, 0)
    screen_slabs = jnp.moveaxis(screened_lesser, 2, 0)

    def convolve_slab(pair):
        return convolve_energy(pair[0], pair[1])

    sigma = lax.map(convolve_slab, (lesser_slabs, screen_slabs))
    sigma_energy = jnp.moveaxis(sigma, 2, 0)
    green_energy = jnp.moveaxis(green_retarded, (1, 2), (0, 1))
    coupling_slabs = jnp.moveaxis(coupling, 1, 0)

    def sweep(pair):
        greens, sigmas = pair

        def advance(state, item):
            green, sigma_block, link = item
            kernel_re = lowdot(green[0], link[0]) - lowdot(green[1], link[1])
            kernel_im = lowdot(green[0], link[1]) + lowdot(green[1], link[0])
            mixed_re = (lowdot(green[0], sigma_block[0]) - lowdot(green[1], sigma_block[1])).astype(jnp.bfloat16)
            mixed_im = (lowdot(green[0], sigma_block[1]) + lowdot(green[1], sigma_block[0])).astype(jnp.bfloat16)
            source_re = lowdot(mixed_re, green[0].T) + lowdot(mixed_im, green[1].T)
            source_im = lowdot(mixed_im, green[0].T) - lowdot(mixed_re, green[1].T)
            updated = congruence((kernel_re, kernel_im), state, (source_re, source_im))
            return updated, jnp.stack(updated)

        blank_block = jnp.zeros((NORB, NORB), jnp.float32)
        final_state, states = lax.scan(advance, (blank_block, blank_block), (greens, sigmas, coupling_slabs))
        return states

    result = lax.map(sweep, (green_energy, sigma_energy))
    return jnp.moveaxis(result, 2, 0)
```

```python
import jax
import jax.numpy as jnp
from jax import lax
from jax.experimental import pallas as pl
from jax.experimental.pallas import tpu as pltpu
from jax.sharding import PartitionSpec as P

F32 = jnp.float32
BF16 = jnp.bfloat16
NORB = 256
POINTS = 16
MIDDLE = POINTS // 2
PEERS = 8
STRIPE = NORB // PEERS
SLABS = 4
EN = 2
SIDE = 4
MESH = pl.DeviceIdType.MESH


def nn(a, b):
    return lax.dot_general(a, b, (((1,), (0,)), ((), ())), preferred_element_type=F32)


def nt(a, b):
    return lax.dot_general(a, b, (((1,), (1,)), ((), ())), preferred_element_type=F32)


def rows(pair):
    return pair.reshape(2 * NORB, NORB)


def left(x3, re, im):
    return nn(rows(x3[1:3]), re) + nn(rows(x3[0:2]), im)


def right(i3, x3):
    return nt(rows(i3[1:3]), x3[1]) + nt(rows(i3[0:2]), x3[0])


def split(value):
    high = value.astype(BF16)
    low = (value - high.astype(F32)).astype(BF16)
    return high, low


def put3(ref, pair):
    ref[1:3] = pair.reshape(2, NORB, NORB)
    ref[0] = -pair[NORB:]


def product(xh, xl, ch, cl):
    total = left(xh, ch[:NORB], ch[NORB:]) + left(xh, cl[:NORB], cl[NORB:])
    if xl is not None:
        total = total + left(xl, ch[:NORB], ch[NORB:])
    return total


def congruence(xh, xl, state, ih, il):
    high, low = split(state)
    inner = product(xh, xl, high, low)
    high, low = split(inner)
    put3(ih, high)
    put3(il, low)
    total = right(ih, xh) + right(il, xh)
    if xl is not None:
        total = total + right(ih, xl)
    return total


def kernel(
    g_hbm, w_hbm, r_hbm, t_hbm, out_hbm,
    gbuf, wbuf, sig, smat, g3, coup, kh, kl, ph, pw, qh, ql, bst,
    mh, ml, nh, nl, arow, rrow, zh, zl, pre, ih, il, gf, wf,
    fs, fr, rs, rr, ms, mr, ns, nr, asend, arecv, xs, xr, ld, od,
):
    slab = lax.axis_index("slab")
    me = lax.axis_index("energy")
    x = slab // SIDE
    z = slab % SIDE

    def energy_peer(k):
        return {"energy": (me + k) % PEERS}

    def z_peer(k):
        return {"slab": x * SIDE + (z + k) % SIDE}

    def x_peer(k):
        return {"slab": ((x + k) % SIDE) * SIDE + z}

    barrier = pltpu.get_barrier_semaphore()
    for k in range(1, PEERS):
        pl.semaphore_signal(barrier, inc=1, device_id=energy_peer(k), device_id_type=MESH)
    for k in range(1, SIDE):
        pl.semaphore_signal(barrier, inc=1, device_id=z_peer(k), device_id_type=MESH)
        pl.semaphore_signal(barrier, inc=1, device_id=x_peer(k), device_id_type=MESH)

    loads = []
    for e in range(EN):
        for s in range(SLABS):
            cp = pltpu.make_async_copy(r_hbm.at[:, e, s], g3.at[e, s, pl.ds(1, 2)], ld.at[e, s])
            cp.start()
            loads.append(cp)
    cp = pltpu.make_async_copy(t_hbm, coup, ld.at[0, SLABS])
    cp.start()
    loads.append(cp)

    def stripe(p):
        return pl.ds(pl.multiple_of(p * STRIPE, STRIPE), STRIPE)

    own = pl.ds(2 * me, EN)
    arrays = ((g_hbm, gbuf), (w_hbm, wbuf))

    def local_stripe(a, s):
        return pltpu.make_async_copy(
            arrays[a][0].at[:, :, s, stripe(me)], arrays[a][1].at[s, :, own], fr.at[a, s, 0]
        )

    def forward(a, s, k):
        p = (me + k) % PEERS
        return pltpu.make_async_remote_copy(
            src_ref=arrays[a][0].at[:, :, s, stripe(p)],
            dst_ref=arrays[a][1].at[s, :, own],
            send_sem=fs.at[a, s, k],
            recv_sem=fr.at[a, s, k],
            device_id={"energy": p},
            device_id_type=MESH,
        )

    pl.semaphore_wait(barrier, PEERS - 1 + 2 * (SIDE - 1))
    for s in range(SLABS):
        for k in range(1, PEERS):
            for a in range(2):
                forward(a, s, k).start()
        for a in range(2):
            local_stripe(a, s).start()

    def gather(k, source, target, send, recv, peer):
        return pltpu.make_async_remote_copy(
            src_ref=source, dst_ref=target, send_sem=send, recv_sem=recv,
            device_id=peer, device_id_type=MESH,
        )

    def send_m(e, k, i):
        view = (mh, ml)[i].at[z, e, pl.ds(1, 2)]
        return gather(k, view, view, ms.at[i, e, k], mr.at[i, e, k], z_peer(k))

    def send_n(e, k, i):
        view = (nh, nl)[i].at[x, e, pl.ds(1, 2)]
        return gather(k, view, view, ns.at[i, e, k], nr.at[i, e, k], x_peer(k))

    def upward(act):
        for k in range(1, SIDE):
            pl.when(x + k < SIDE)(lambda k=k: act(k))

    def from_below(act):
        for k in range(1, SIDE):
            pl.when(x - k >= 0)(lambda k=k: act(k))

    def send_a(e, k):
        view = arow.at[z, e]
        return gather(k, view, view, asend.at[e, k], arecv.at[e, k], z_peer(k))

    def send_r(e, k):
        view = rrow.at[x, e]
        return gather(k, view, view, xs.at[e, k], xr.at[e, k], x_peer(k))

    for cp in loads:
        cp.wait()

    @pl.loop(0, EN)
    def _(e):
        @pl.loop(0, SLABS)
        def _(s):
            g3[e, s, 0] = -g3[e, s, 2]
            high, low = split(left(g3[e, s], coup[0, s], coup[1, s]))
            put3(kh.at[e, s], high)
            put3(kl.at[e, s], low)

        ph[e, 0] = kh[e, 0]
        pw[e, 0] = kl[e, 0]

        @pl.loop(1, SLABS)
        def _(s):
            value = product(kh[e, s], kl[e, s], rows(ph[e, s - 1, 1:3]), rows(pw[e, s - 1, 1:3]))
            high, low = split(value)
            put3(ph.at[e, s], high)
            put3(pw.at[e, s], low)

        mh[z, e] = ph[e, SLABS - 1]
        ml[z, e] = pw[e, SLABS - 1]
        for i in range(2):
            for k in range(1, SIDE):
                send_m(e, k, i).start()

    def convolve(s):
        for a in range(2):
            local_stripe(a, s).wait()
        for k in range(1, PEERS):
            for a in range(2):
                forward(a, s, k).wait_recv()

        @pl.loop(0, STRIPE // 16)
        def _(tr):
            @pl.loop(0, NORB // 128)
            def _(tc):
                rr_ = pl.ds(pl.multiple_of(tr * 16, 16), 16)
                cc_ = pl.ds(pl.multiple_of(tc * 128, 128), 128)
                for part in range(2):
                    for m in range(POINTS):
                        gf[part, m] = gbuf[s, part, m, rr_, cc_].astype(F32)
                        wf[part, m] = wbuf[s, part, m, rr_, cc_].astype(F32)
                for n in range(POINTS):
                    re = None
                    im = None
                    for m in range(max(0, n + MIDDLE + 1 - POINTS), min(POINTS, n + MIDDLE + 1)):
                        l = n - m + MIDDLE
                        a, b = gf[0, m], gf[1, m]
                        c, d = wf[0, l], wf[1, l]
                        r = a * c - b * d
                        i = a * d + b * c
                        re = r if re is None else re + r
                        im = i if im is None else im + i
                    sig[s, 0, n, rr_, cc_] = (im * (-1.0 / POINTS)).astype(BF16)
                    sig[s, 1, n, rr_, cc_] = (re * (1.0 / POINTS)).astype(BF16)

    parts = (pl.ds(0, SLABS - 1), pl.ds(SLABS - 1, 1))

    def giveback(e, part, k):
        p = (me + k) % PEERS
        return pltpu.make_async_remote_copy(
            src_ref=sig.at[parts[part], :, 2 * p + e],
            dst_ref=smat.at[e, parts[part], :, stripe(me)],
            send_sem=rs.at[e, part, k],
            recv_sem=rr.at[e, part, k],
            device_id={"energy": p},
            device_id_type=MESH,
        )

    def keep(e, part):
        return pltpu.make_async_copy(
            sig.at[parts[part], :, 2 * me + e], smat.at[e, parts[part], :, stripe(me)], rr.at[e, part, 0]
        )

    def row_products(e):
        for i in range(2):
            for k in range(1, SIDE):
                send_m(e, k, i).wait_recv()
        eye = (
            lax.broadcasted_iota(jnp.int32, (NORB, NORB), 0)
            == lax.broadcasted_iota(jnp.int32, (NORB, NORB), 1)
        )
        zh[0, 0] = jnp.zeros((NORB, NORB), BF16)
        zh[0, 1] = jnp.where(eye, 1.0, 0.0).astype(BF16)
        zh[0, 2] = jnp.zeros((NORB, NORB), BF16)
        zl[0] = jnp.zeros((3, NORB, NORB), BF16)

        @pl.loop(0, SIDE)
        def _(j):
            mh[j, e, 0] = -mh[j, e, 2]
            ml[j, e, 0] = -ml[j, e, 2]
            value = product(mh[j, e], ml[j, e], rows(zh[j, 1:3]), rows(zl[j, 1:3]))
            high, low = split(value)
            put3(zh.at[j + 1], high)
            put3(zl.at[j + 1], low)

        nh[x, e] = zh[SIDE]
        nl[x, e] = zl[SIDE]

        @pl.when(x > 0)
        def _():
            for i in range(2):
                upward(lambda k: send_n(e, k, i).start())

        @pl.loop(0, SLABS)
        def _(s):
            value = product(ph[e, s], pw[e, s], rows(zh[z, 1:3]), rows(zl[z, 1:3]))
            high, low = split(value)
            put3(qh.at[e, s], high)
            put3(ql.at[e, s], low)

    @pl.loop(0, SLABS - 2)
    def _(s):
        convolve(s)

    row_products(0)
    convolve(SLABS - 2)
    for k in range(1, PEERS):
        giveback(0, 0, k).start()
    keep(0, 0).start()
    convolve(SLABS - 1)
    for e, part in ((0, 1), (1, 0), (1, 1)):
        for k in range(1, PEERS):
            giveback(e, part, k).start()
        keep(e, part).start()
    row_products(1)

    @pl.loop(0, EN)
    def _(e):
        for part in range(2):
            keep(e, part).wait()
            for k in range(1, PEERS):
                giveback(e, part, k).wait_recv()

        @pl.loop(0, SLABS)
        def _(s):
            mixed = left(g3[e, s], smat[e, s, 0], smat[e, s, 1]).astype(BF16)
            put3(ih, mixed)
            bst[e, s] = right(ih, g3[e, s]).reshape(2, NORB, NORB)

        @pl.loop(1, SLABS)
        def _(s):
            value = congruence(kh[e, s], kl[e, s], rows(bst[e, s - 1]), ih, il)
            bst[e, s] += value.reshape(2, NORB, NORB)

        arow[z, e] = bst[e, SLABS - 1].astype(BF16)
        for k in range(1, SIDE):
            send_a(e, k).start()

    def scan(e, high, low, values, count):
        pre[0] = jnp.zeros((2, NORB, NORB), F32)
        pre[1] = values[0, e].astype(F32)

        @pl.loop(1, count)
        def _(j):
            value = congruence(high[j, e], low[j, e], rows(pre[j]), ih, il)
            pre[j + 1] = value.reshape(2, NORB, NORB) + values[j, e].astype(F32)

    def spread(e, high, low, index):
        @pl.loop(0, SLABS)
        def _(s):
            value = congruence(high[e, s], low[e, s], rows(pre[index]), ih, il)
            bst[e, s] += value.reshape(2, NORB, NORB)

    @pl.loop(0, EN)
    def _(e):
        for k in range(1, SIDE):
            send_a(e, k).wait_recv()
        scan(e, mh, ml, arow, SIDE)
        rrow[x, e] = pre[SIDE].astype(BF16)
        upward(lambda k: send_r(e, k).start())
        spread(e, ph, pw, z)

    def store(e, s):
        return pltpu.make_async_copy(bst.at[e, s], out_hbm.at[:, e, s], od.at[e, s])

    @pl.loop(0, EN)
    def _(e):
        from_below(lambda k: send_r(e, k).wait_recv())

        @pl.when(x > 0)
        def _():
            for k in range(1, SIDE - 1):

                @pl.when(x - k > 0)
                def _(k=k):
                    for i in range(2):
                        send_n(e, k, i).wait_recv()

            pre[1] = rrow[0, e].astype(F32)

            @pl.loop(1, x)
            def _(j):
                nh[j, e, 0] = -nh[j, e, 2]
                nl[j, e, 0] = -nl[j, e, 2]
                value = congruence(nh[j, e], nl[j, e], rows(pre[j]), ih, il)
                pre[j + 1] = value.reshape(2, NORB, NORB) + rrow[j, e].astype(F32)

            spread(e, qh, ql, x)

        for s in range(SLABS):
            store(e, s).start()

    for e in range(EN):
        for s in range(SLABS):
            store(e, s).wait()
        for k in range(1, SIDE):
            send_m(e, k, 0).wait_send()
            send_m(e, k, 1).wait_send()
            send_a(e, k).wait_send()
        upward(lambda k: send_r(e, k).wait_send())

        @pl.when(x > 0)
        def _(e=e):
            for i in range(2):
                upward(lambda k: send_n(e, k, i).wait_send())

        for part in range(2):
            for k in range(1, PEERS):
                giveback(e, part, k).wait_send()
    for s in range(SLABS):
        for k in range(1, PEERS):
            for a in range(2):
                forward(a, s, k).wait_send()


def per_device(green_lesser, screened_lesser, green_retarded, coupling):
    block = (NORB, NORB)
    dma = pltpu.SemaphoreType.DMA
    return pl.pallas_call(
        kernel,
        out_shape=jax.ShapeDtypeStruct((2, EN, SLABS) + block, F32),
        in_specs=[pl.BlockSpec(memory_space=pl.ANY)] * 4,
        out_specs=pl.BlockSpec(memory_space=pl.ANY),
        scratch_shapes=[
            pltpu.VMEM((SLABS, 2, POINTS, STRIPE, NORB), BF16),
            pltpu.VMEM((SLABS, 2, POINTS, STRIPE, NORB), BF16),
            pltpu.VMEM((SLABS, 2, POINTS, STRIPE, NORB), BF16),
            pltpu.VMEM((EN, SLABS, 2) + block, BF16),
            pltpu.VMEM((EN, SLABS, 3) + block, BF16),
            pltpu.VMEM((2, SLABS) + block, BF16),
            pltpu.VMEM((EN, SLABS, 3) + block, BF16),
            pltpu.VMEM((EN, SLABS, 3) + block, BF16),
            pltpu.VMEM((EN, SLABS, 3) + block, BF16),
            pltpu.VMEM((EN, SLABS, 3) + block, BF16),
            pltpu.VMEM((EN, SLABS, 3) + block, BF16),
            pltpu.VMEM((EN, SLABS, 3) + block, BF16),
            pltpu.VMEM((EN, SLABS, 2) + block, F32),
            pltpu.VMEM((SIDE, EN, 3) + block, BF16),
            pltpu.VMEM((SIDE, EN, 3) + block, BF16),
            pltpu.VMEM((SIDE, EN, 3) + block, BF16),
            pltpu.VMEM((SIDE, EN, 3) + block, BF16),
            pltpu.VMEM((SIDE, EN, 2) + block, BF16),
            pltpu.VMEM((SIDE, EN, 2) + block, BF16),
            pltpu.VMEM((SIDE + 1, 3) + block, BF16),
            pltpu.VMEM((SIDE + 1, 3) + block, BF16),
            pltpu.VMEM((SIDE + 1, 2) + block, F32),
            pltpu.VMEM((3,) + block, BF16),
            pltpu.VMEM((3,) + block, BF16),
            pltpu.VMEM((2, POINTS, 16, 128), F32),
            pltpu.VMEM((2, POINTS, 16, 128), F32),
            dma((2, SLABS, PEERS)),
            dma((2, SLABS, PEERS)),
            dma((EN, 2, PEERS)),
            dma((EN, 2, PEERS)),
            dma((2, EN, SIDE)),
            dma((2, EN, SIDE)),
            dma((2, EN, SIDE)),
            dma((2, EN, SIDE)),
            dma((EN, SIDE)),
            dma((EN, SIDE)),
            dma((EN, SIDE)),
            dma((EN, SIDE)),
            dma((EN, SLABS + 1)),
            dma((EN, SLABS)),
        ],
        compiler_params=pltpu.CompilerParams(
            collective_id=0, has_side_effects=True, vmem_limit_bytes=63000 * 1024
        ),
        name="born_step",
    )(green_lesser, screened_lesser, green_retarded, coupling)


def solution(mesh):
    placed = (
        P(None, "energy", "slab", None, None),
        P(None, "energy", "slab", None, None),
        P(None, "energy", "slab", None, None),
        P(None, "slab", None, None),
    )
    return jax.shard_map(
        per_device,
        mesh=mesh,
        in_specs=placed,
        out_specs=P(None, "energy", "slab", None, None),
        check_vma=False,
    )
```

```python
import jax
import jax.numpy as jnp
from jax import lax
from jax.experimental import pallas as pl
from jax.experimental.pallas import tpu as pltpu
from jax.sharding import PartitionSpec as P

F32 = jnp.float32
BF16 = jnp.bfloat16
NORB = 256
POINTS = 16
MIDDLE = POINTS // 2
PEERS = 8
STRIPE = NORB // PEERS
SLABS = 4
EN = 2
SIDE = 4
MESH = pl.DeviceIdType.MESH


def nn(a, b):
    return lax.dot_general(a, b, (((1,), (0,)), ((), ())), preferred_element_type=F32)


def nt(a, b):
    return lax.dot_general(a, b, (((1,), (1,)), ((), ())), preferred_element_type=F32)


def rows(pair):
    return pair.reshape(2 * NORB, NORB)


def left(x3, re, im):
    return nn(rows(x3[1:3]), re) + nn(rows(x3[0:2]), im)


def right(i3, x3):
    return nt(rows(i3[1:3]), x3[1]) + nt(rows(i3[0:2]), x3[0])


def split(value):
    high = value.astype(BF16)
    low = (value - high.astype(F32)).astype(BF16)
    return high, low


def put3(ref, pair):
    ref[1:3] = pair.reshape(2, NORB, NORB)
    ref[0] = -pair[NORB:]


def product(xh, xl, ch, cl):
    total = left(xh, ch[:NORB], ch[NORB:]) + left(xl, ch[:NORB], ch[NORB:])
    if cl is not None:
        total = total + left(xh, cl[:NORB], cl[NORB:])
    return total


def congruence(xh, xl, state, ih, il, exact=False):
    high, low = split(state)
    inner = product(xh, xl, high, None if exact else low)
    high, low = split(inner)
    put3(ih, high)
    put3(il, low)
    return right(ih, xh) + right(il, xh) + right(ih, xl)


def kernel(
    g_hbm, w_hbm, r_hbm, t_hbm, out_hbm,
    gbuf, wbuf, sig, smat, g3, coup, kh, kl, ph, pw, yh, yl, bst, cin,
    mh, ml, nh, nl, arow, rrow, zh, zl, pre, ih, il, gf, wf,
    fs, fr, rs, rr, ms, mr, ns, nr, asend, arecv, xs, xr, ld, od,
):
    slab = lax.axis_index("slab")
    me = lax.axis_index("energy")
    x = slab // SIDE
    z = slab % SIDE

    def energy_peer(k):
        return {"energy": (me + k) % PEERS}

    def z_peer(k):
        return {"slab": x * SIDE + (z + k) % SIDE}

    def x_peer(k):
        return {"slab": ((x + k) % SIDE) * SIDE + z}

    barrier = pltpu.get_barrier_semaphore()
    for k in range(1, PEERS):
        pl.semaphore_signal(barrier, inc=1, device_id=energy_peer(k), device_id_type=MESH)
    for k in range(1, SIDE):
        pl.semaphore_signal(barrier, inc=1, device_id=z_peer(k), device_id_type=MESH)
        pl.semaphore_signal(barrier, inc=1, device_id=x_peer(k), device_id_type=MESH)

    loads = []
    for e in range(EN):
        for s in range(SLABS):
            cp = pltpu.make_async_copy(r_hbm.at[:, e, s], g3.at[e, s, pl.ds(1, 2)], ld.at[e, s])
            cp.start()
            loads.append(cp)
    cp = pltpu.make_async_copy(t_hbm, coup, ld.at[0, SLABS])
    cp.start()
    loads.append(cp)

    def stripe(p):
        return pl.ds(pl.multiple_of(p * STRIPE, STRIPE), STRIPE)

    own = pl.ds(2 * me, EN)
    arrays = ((g_hbm, gbuf), (w_hbm, wbuf))

    def local_stripe(a, s):
        return pltpu.make_async_copy(
            arrays[a][0].at[:, :, s, stripe(me)], arrays[a][1].at[s, :, own], fr.at[a, s, 0]
        )

    def forward(a, s, k):
        p = (me + k) % PEERS
        return pltpu.make_async_remote_copy(
            src_ref=arrays[a][0].at[:, :, s, stripe(p)],
            dst_ref=arrays[a][1].at[s, :, own],
            send_sem=fs.at[a, s, k],
            recv_sem=fr.at[a, s, k],
            device_id={"energy": p},
            device_id_type=MESH,
        )

    pl.semaphore_wait(barrier, PEERS - 1 + 2 * (SIDE - 1))
    for s in range(SLABS):
        for k in range(1, PEERS):
            for a in range(2):
                forward(a, s, k).start()
        for a in range(2):
            local_stripe(a, s).start()

    def gather(k, source, target, send, recv, peer):
        return pltpu.make_async_remote_copy(
            src_ref=source, dst_ref=target, send_sem=send, recv_sem=recv,
            device_id=peer, device_id_type=MESH,
        )

    def send_m(e, k, i):
        view = (mh, ml)[i].at[z, e, pl.ds(1, 2)]
        return gather(k, view, view, ms.at[i, e, k], mr.at[i, e, k], z_peer(k))

    def send_n(e, k, i):
        view = (nh, nl)[i].at[x, e, pl.ds(1, 2)]
        return gather(k, view, view, ns.at[i, e, k], nr.at[i, e, k], x_peer(k))

    def upward(act):
        for k in range(1, SIDE):
            pl.when(x + k < SIDE)(lambda k=k: act(k))

    def send_a(e, k):
        view = arow.at[z, e]
        return gather(k, view, view, asend.at[e, k], arecv.at[e, k], z_peer(k))

    def send_r(e, k):
        view = rrow.at[x, e]
        return gather(k, view, view, xs.at[e, k], xr.at[e, k], x_peer(k))

    for cp in loads:
        cp.wait()

    @pl.loop(0, EN)
    def _(e):
        @pl.loop(0, SLABS)
        def _(s):
            g3[e, s, 0] = -g3[e, s, 2]
            high, low = split(left(g3[e, s], coup[0, s], coup[1, s]))
            put3(kh.at[e, s], high)
            put3(kl.at[e, s], low)

        ph[e, 0] = kh[e, 0]
        pw[e, 0] = kl[e, 0]

        @pl.loop(1, SLABS)
        def _(s):
            value = product(kh[e, s], kl[e, s], rows(ph[e, s - 1, 1:3]), rows(pw[e, s - 1, 1:3]))
            high, low = split(value)
            put3(ph.at[e, s], high)
            put3(pw.at[e, s], low)

        mh[z, e] = ph[e, SLABS - 1]
        ml[z, e] = pw[e, SLABS - 1]
        for i in range(2):
            for k in range(1, SIDE):
                send_m(e, k, i).start()

    def convolve(s):
        for a in range(2):
            local_stripe(a, s).wait()
        for k in range(1, PEERS):
            for a in range(2):
                forward(a, s, k).wait_recv()

        @pl.loop(0, STRIPE // 16)
        def _(tr):
            @pl.loop(0, NORB // 128)
            def _(tc):
                rr_ = pl.ds(pl.multiple_of(tr * 16, 16), 16)
                cc_ = pl.ds(pl.multiple_of(tc * 128, 128), 128)
                for part in range(2):
                    for m in range(POINTS):
                        gf[part, m] = gbuf[s, part, m, rr_, cc_].astype(F32)
                        wf[part, m] = wbuf[s, part, m, rr_, cc_].astype(F32)
                for n in range(POINTS):
                    re = None
                    im = None
                    for m in range(max(0, n + MIDDLE + 1 - POINTS), min(POINTS, n + MIDDLE + 1)):
                        l = n - m + MIDDLE
                        a, b = gf[0, m], gf[1, m]
                        c, d = wf[0, l], wf[1, l]
                        r = a * c - b * d
                        i = a * d + b * c
                        re = r if re is None else re + r
                        im = i if im is None else im + i
                    sig[s, 0, n, rr_, cc_] = (im * (-1.0 / POINTS)).astype(BF16)
                    sig[s, 1, n, rr_, cc_] = (re * (1.0 / POINTS)).astype(BF16)

    parts = (pl.ds(0, SLABS - 1), pl.ds(SLABS - 1, 1))

    def giveback(e, part, k):
        p = (me + k) % PEERS
        return pltpu.make_async_remote_copy(
            src_ref=sig.at[parts[part], :, 2 * p + e],
            dst_ref=smat.at[e, parts[part], :, stripe(me)],
            send_sem=rs.at[e, part, k],
            recv_sem=rr.at[e, part, k],
            device_id={"energy": p},
            device_id_type=MESH,
        )

    def keep(e, part):
        return pltpu.make_async_copy(
            sig.at[parts[part], :, 2 * me + e], smat.at[e, parts[part], :, stripe(me)], rr.at[e, part, 0]
        )

    def row_products(e):
        for i in range(2):
            for k in range(1, SIDE):
                send_m(e, k, i).wait_recv()
        eye = (
            lax.broadcasted_iota(jnp.int32, (NORB, NORB), 0)
            == lax.broadcasted_iota(jnp.int32, (NORB, NORB), 1)
        )
        zh[0, 0] = jnp.zeros((NORB, NORB), BF16)
        zh[0, 1] = jnp.where(eye, 1.0, 0.0).astype(BF16)
        zh[0, 2] = jnp.zeros((NORB, NORB), BF16)
        zl[0] = jnp.zeros((3, NORB, NORB), BF16)

        @pl.loop(0, SIDE)
        def _(j):
            mh[j, e, 0] = -mh[j, e, 2]
            ml[j, e, 0] = -ml[j, e, 2]
            value = product(mh[j, e], ml[j, e], rows(zh[j, 1:3]), rows(zl[j, 1:3]))
            high, low = split(value)
            put3(zh.at[j + 1], high)
            put3(zl.at[j + 1], low)

        nh[x, e] = zh[SIDE]
        nl[x, e] = zl[SIDE]

        @pl.when(x > 0)
        def _():
            for i in range(2):
                upward(lambda k: send_n(e, k, i).start())

        yh[e] = zh[z]
        yl[e] = zl[z]

    @pl.loop(0, SLABS - 2)
    def _(s):
        convolve(s)

    row_products(0)
    convolve(SLABS - 2)
    for k in range(1, PEERS):
        giveback(0, 0, k).start()
    keep(0, 0).start()
    convolve(SLABS - 1)
    for e, part in ((0, 1), (1, 0), (1, 1)):
        for k in range(1, PEERS):
            giveback(e, part, k).start()
        keep(e, part).start()
    row_products(1)

    def returned(e, part):
        keep(e, part).wait()
        for k in range(1, PEERS):
            giveback(e, part, k).wait_recv()

    @pl.loop(0, EN)
    def _(e):
        returned(e, 0)

        @pl.loop(0, SLABS)
        def _(s):
            @pl.when(s == SLABS - 1)
            def _():
                returned(e, 1)

            mixed = left(g3[e, s], smat[e, s, 0], smat[e, s, 1]).astype(BF16)
            put3(ih, mixed)
            bst[e, s] = right(ih, g3[e, s]).reshape(2, NORB, NORB)

            @pl.when(s > 0)
            def _():
                value = congruence(kh[e, s], kl[e, s], rows(bst[e, s - 1]), ih, il)
                bst[e, s] += value.reshape(2, NORB, NORB)

        arow[z, e] = bst[e, SLABS - 1].astype(BF16)
        for k in (2, 1, 3):
            send_a(e, k).start()

    top = jnp.where(x < SIDE - 1, SIDE, jnp.maximum(z, 1))

    @pl.loop(0, EN)
    def _(e):
        def arrived(j):
            k = (z - j + SIDE) % SIDE

            @pl.when(k > 0)
            def _():
                send_a(e, k).wait_recv()

        def step(j, exact):
            value = congruence(mh[j, e], ml[j, e], rows(pre[j]), ih, il, exact)
            pre[j + 1] = value.reshape(2, NORB, NORB)
            arrived(j)
            pre[j + 1] += arow[j, e].astype(F32)

        pre[0] = jnp.zeros((2, NORB, NORB), F32)
        arrived(0)
        pre[1] = arow[0, e].astype(F32)

        @pl.when(top > 1)
        def _():
            step(1, True)

            @pl.loop(2, top)
            def _(j):
                step(j, False)

        @pl.loop(top, SIDE)
        def _(j):
            arrived(j)

        @pl.when(x < SIDE - 1)
        def _():
            rrow[x, e] = pre[SIDE].astype(BF16)
            for k in range(SIDE - 1, 0, -1):

                @pl.when(x + k < SIDE)
                def _(k=k):
                    send_r(e, k).start()

        cin[e] = pre[z]

    def store(e, s):
        return pltpu.make_async_copy(bst.at[e, s], out_hbm.at[:, e, s], od.at[e, s])

    @pl.loop(0, EN)
    def _(e):
        def step(j, exact):
            for i in range(2):
                send_n(e, x - j, i).wait_recv()
            nh[j, e, 0] = -nh[j, e, 2]
            nl[j, e, 0] = -nl[j, e, 2]
            value = congruence(nh[j, e], nl[j, e], rows(pre[j]), ih, il, exact)
            pre[j + 1] = value.reshape(2, NORB, NORB)
            send_r(e, x - j).wait_recv()
            pre[j + 1] += rrow[j, e].astype(F32)

        @pl.when(x > 0)
        def _():
            send_r(e, x).wait_recv()
            pre[1] = rrow[0, e].astype(F32)

            @pl.when(x > 1)
            def _():
                step(1, True)

                @pl.loop(2, x)
                def _(j):
                    step(j, False)

            value = congruence(yh[e], yl[e], rows(pre[x]), ih, il)
            cin[e] += value.reshape(2, NORB, NORB)

        @pl.loop(0, SLABS)
        def _(s):
            @pl.when(slab > 0)
            def _():
                value = congruence(ph[e, s], pw[e, s], rows(cin[e]), ih, il)
                bst[e, s] += value.reshape(2, NORB, NORB)

            store(e, s).start()

    for e in range(EN):
        for s in range(SLABS):
            store(e, s).wait()
        for k in range(1, SIDE):
            send_m(e, k, 0).wait_send()
            send_m(e, k, 1).wait_send()
            send_a(e, k).wait_send()
        upward(lambda k: send_r(e, k).wait_send())

        @pl.when(x > 0)
        def _(e=e):
            for i in range(2):
                upward(lambda k: send_n(e, k, i).wait_send())

        for part in range(2):
            for k in range(1, PEERS):
                giveback(e, part, k).wait_send()
    for s in range(SLABS):
        for k in range(1, PEERS):
            for a in range(2):
                forward(a, s, k).wait_send()


def per_device(green_lesser, screened_lesser, green_retarded, coupling):
    block = (NORB, NORB)
    dma = pltpu.SemaphoreType.DMA
    return pl.pallas_call(
        kernel,
        out_shape=jax.ShapeDtypeStruct((2, EN, SLABS) + block, F32),
        in_specs=[pl.BlockSpec(memory_space=pl.ANY)] * 4,
        out_specs=pl.BlockSpec(memory_space=pl.ANY),
        scratch_shapes=[
            pltpu.VMEM((SLABS, 2, POINTS, STRIPE, NORB), BF16),
            pltpu.VMEM((SLABS, 2, POINTS, STRIPE, NORB), BF16),
            pltpu.VMEM((SLABS, 2, POINTS, STRIPE, NORB), BF16),
            pltpu.VMEM((EN, SLABS, 2) + block, BF16),
            pltpu.VMEM((EN, SLABS, 3) + block, BF16),
            pltpu.VMEM((2, SLABS) + block, BF16),
            pltpu.VMEM((EN, SLABS, 3) + block, BF16),
            pltpu.VMEM((EN, SLABS, 3) + block, BF16),
            pltpu.VMEM((EN, SLABS, 3) + block, BF16),
            pltpu.VMEM((EN, SLABS, 3) + block, BF16),
            pltpu.VMEM((EN, 3) + block, BF16),
            pltpu.VMEM((EN, 3) + block, BF16),
            pltpu.VMEM((EN, SLABS, 2) + block, F32),
            pltpu.VMEM((EN, 2) + block, F32),
            pltpu.VMEM((SIDE, EN, 3) + block, BF16),
            pltpu.VMEM((SIDE, EN, 3) + block, BF16),
            pltpu.VMEM((SIDE, EN, 3) + block, BF16),
            pltpu.VMEM((SIDE, EN, 3) + block, BF16),
            pltpu.VMEM((SIDE, EN, 2) + block, BF16),
            pltpu.VMEM((SIDE, EN, 2) + block, BF16),
            pltpu.VMEM((SIDE + 1, 3) + block, BF16),
            pltpu.VMEM((SIDE + 1, 3) + block, BF16),
            pltpu.VMEM((SIDE + 1, 2) + block, F32),
            pltpu.VMEM((3,) + block, BF16),
            pltpu.VMEM((3,) + block, BF16),
            pltpu.VMEM((2, POINTS, 16, 128), F32),
            pltpu.VMEM((2, POINTS, 16, 128), F32),
            dma((2, SLABS, PEERS)),
            dma((2, SLABS, PEERS)),
            dma((EN, 2, PEERS)),
            dma((EN, 2, PEERS)),
            dma((2, EN, SIDE)),
            dma((2, EN, SIDE)),
            dma((2, EN, SIDE)),
            dma((2, EN, SIDE)),
            dma((EN, SIDE)),
            dma((EN, SIDE)),
            dma((EN, SIDE)),
            dma((EN, SIDE)),
            dma((EN, SLABS + 1)),
            dma((EN, SLABS)),
        ],
        compiler_params=pltpu.CompilerParams(
            collective_id=0, has_side_effects=True, vmem_limit_bytes=63000 * 1024
        ),
        name="born_step",
    )(green_lesser, screened_lesser, green_retarded, coupling)


def solution(mesh):
    placed = (
        P(None, "energy", "slab", None, None),
        P(None, "energy", "slab", None, None),
        P(None, "energy", "slab", None, None),
        P(None, "slab", None, None),
    )
    return jax.shard_map(
        per_device,
        mesh=mesh,
        in_specs=placed,
        out_specs=P(None, "energy", "slab", None, None),
        check_vma=False,
    )
```

```python
import jax
import jax.numpy as jnp
from jax import lax
from jax.experimental import pallas as pl
from jax.experimental.pallas import tpu as pltpu
from jax.sharding import PartitionSpec as P

F32 = jnp.float32
BF16 = jnp.bfloat16
NORB = 256
POINTS = 16
MIDDLE = POINTS // 2
PEERS = 8
STRIPE = NORB // PEERS
SLABS = 4
EN = 2
SIDE = 4
MESH = pl.DeviceIdType.MESH


def nn(a, b):
    return lax.dot_general(a, b, (((1,), (0,)), ((), ())), preferred_element_type=F32)


def nt(a, b):
    return lax.dot_general(a, b, (((1,), (1,)), ((), ())), preferred_element_type=F32)


def rows(pair):
    return pair.reshape(2 * NORB, NORB)


def left(x3, re, im):
    return nn(rows(x3[1:3]), re) + nn(rows(x3[0:2]), im)


def right(i3, x3):
    return nt(rows(i3[1:3]), x3[1]) + nt(rows(i3[0:2]), x3[0])


def split(value):
    high = value.astype(BF16)
    low = (value - high.astype(F32)).astype(BF16)
    return high, low


def put3(ref, pair):
    ref[1:3] = pair.reshape(2, NORB, NORB)
    ref[0] = -pair[NORB:]


def product(xh, xl, ch, cl):
    total = left(xh, ch[:NORB], ch[NORB:]) + left(xl, ch[:NORB], ch[NORB:])
    if cl is not None:
        total = total + left(xh, cl[:NORB], cl[NORB:])
    return total


def congruence(xh, xl, state, ih, il, exact=False, brief=False):
    high, low = (state.astype(BF16), None) if exact else split(state)
    inner = product(xh, xl, high, low)
    if brief:
        put3(ih, inner.astype(BF16))
        return right(ih, xh) + right(ih, xl)
    high, low = split(inner)
    put3(ih, high)
    put3(il, low)
    return right(ih, xh) + right(il, xh) + right(ih, xl)


def kernel(
    g_hbm, w_hbm, r_hbm, t_hbm, out_hbm,
    gbuf, wbuf, sig, smat, g3, coup, kh, kl, ph, pw, yh, yl, wh, wl, bst, cin,
    mh, ml, nh, nl, arow, rrow, zh, zl, pre, ih, il, gf, wf,
    fs, fr, rs, rr, ms, mr, ns, nr, asend, arecv, xs, xr, ld, od,
):
    slab = lax.axis_index("slab")
    me = lax.axis_index("energy")
    x = slab // SIDE
    z = slab % SIDE

    def energy_peer(k):
        return {"energy": (me + k) % PEERS}

    def z_peer(k):
        return {"slab": x * SIDE + (z + k) % SIDE}

    def x_peer(k):
        return {"slab": ((x + k) % SIDE) * SIDE + z}

    barrier = pltpu.get_barrier_semaphore()
    for k in range(1, PEERS):
        pl.semaphore_signal(barrier, inc=1, device_id=energy_peer(k), device_id_type=MESH)
    for k in range(1, SIDE):
        pl.semaphore_signal(barrier, inc=1, device_id=z_peer(k), device_id_type=MESH)
        pl.semaphore_signal(barrier, inc=1, device_id=x_peer(k), device_id_type=MESH)

    loads = []
    for e in range(EN):
        for s in range(SLABS):
            cp = pltpu.make_async_copy(r_hbm.at[:, e, s], g3.at[e, s, pl.ds(1, 2)], ld.at[e, s])
            cp.start()
            loads.append(cp)
    cp = pltpu.make_async_copy(t_hbm, coup, ld.at[0, SLABS])
    cp.start()
    loads.append(cp)

    def stripe(p):
        return pl.ds(pl.multiple_of(p * STRIPE, STRIPE), STRIPE)

    own = pl.ds(2 * me, EN)
    arrays = ((g_hbm, gbuf), (w_hbm, wbuf))

    def local_stripe(a, s):
        return pltpu.make_async_copy(
            arrays[a][0].at[:, :, s, stripe(me)], arrays[a][1].at[s, :, own], fr.at[a, s, 0]
        )

    def forward(a, s, k):
        p = (me + k) % PEERS
        return pltpu.make_async_remote_copy(
            src_ref=arrays[a][0].at[:, :, s, stripe(p)],
            dst_ref=arrays[a][1].at[s, :, own],
            send_sem=fs.at[a, s, k],
            recv_sem=fr.at[a, s, k],
            device_id={"energy": p},
            device_id_type=MESH,
        )

    pl.semaphore_wait(barrier, PEERS - 1 + 2 * (SIDE - 1))
    for s in range(SLABS):
        for k in range(1, PEERS):
            for a in range(2):
                forward(a, s, k).start()
        for a in range(2):
            local_stripe(a, s).start()

    def gather(k, source, target, send, recv, peer):
        return pltpu.make_async_remote_copy(
            src_ref=source, dst_ref=target, send_sem=send, recv_sem=recv,
            device_id=peer, device_id_type=MESH,
        )

    def send_m(e, k, i):
        view = (mh, ml)[i].at[z, e, pl.ds(1, 2)]
        return gather(k, view, view, ms.at[i, e, k], mr.at[i, e, k], z_peer(k))

    def send_n(e, k, i):
        view = (nh, nl)[i].at[x, e, pl.ds(1, 2)]
        return gather(k, view, view, ns.at[i, e, k], nr.at[i, e, k], x_peer(k))

    def upward(act):
        for k in range(1, SIDE):
            pl.when(x + k < SIDE)(lambda k=k: act(k))

    def send_a(e, k):
        view = arow.at[z, e]
        return gather(k, view, view, asend.at[e, k], arecv.at[e, k], z_peer(k))

    def send_r(e, k):
        view = rrow.at[x, e]
        return gather(k, view, view, xs.at[e, k], xr.at[e, k], x_peer(k))

    for cp in loads:
        cp.wait()

    @pl.loop(0, EN)
    def _(e):
        @pl.loop(0, SLABS)
        def _(s):
            g3[e, s, 0] = -g3[e, s, 2]
            high, low = split(left(g3[e, s], coup[0, s], coup[1, s]))
            put3(kh.at[e, s], high)
            put3(kl.at[e, s], low)

        ph[e, 0] = kh[e, 0]
        pw[e, 0] = kl[e, 0]

        @pl.loop(1, SLABS)
        def _(s):
            value = product(kh[e, s], kl[e, s], rows(ph[e, s - 1, 1:3]), rows(pw[e, s - 1, 1:3]))
            high, low = split(value)
            put3(ph.at[e, s], high)
            put3(pw.at[e, s], low)

        mh[z, e] = ph[e, SLABS - 1]
        ml[z, e] = pw[e, SLABS - 1]
        for i in range(2):
            for k in range(1, SIDE):
                send_m(e, k, i).start()

    def convolve(s):
        for a in range(2):
            local_stripe(a, s).wait()
        for k in range(1, PEERS):
            for a in range(2):
                forward(a, s, k).wait_recv()

        @pl.loop(0, STRIPE // 16)
        def _(tr):
            @pl.loop(0, NORB // 128)
            def _(tc):
                rr_ = pl.ds(pl.multiple_of(tr * 16, 16), 16)
                cc_ = pl.ds(pl.multiple_of(tc * 128, 128), 128)
                for part in range(2):
                    for m in range(POINTS):
                        gf[part, m] = gbuf[s, part, m, rr_, cc_].astype(F32)
                        wf[part, m] = wbuf[s, part, m, rr_, cc_].astype(F32)
                for n in range(POINTS):
                    re = None
                    im = None
                    for m in range(max(0, n + MIDDLE + 1 - POINTS), min(POINTS, n + MIDDLE + 1)):
                        l = n - m + MIDDLE
                        a, b = gf[0, m], gf[1, m]
                        c, d = wf[0, l], wf[1, l]
                        r = a * c - b * d
                        i = a * d + b * c
                        re = r if re is None else re + r
                        im = i if im is None else im + i
                    sig[s, 0, n, rr_, cc_] = (im * (-1.0 / POINTS)).astype(BF16)
                    sig[s, 1, n, rr_, cc_] = (re * (1.0 / POINTS)).astype(BF16)

    def giveback(e, s, k):
        p = (me + k) % PEERS
        return pltpu.make_async_remote_copy(
            src_ref=sig.at[s, :, 2 * p + e],
            dst_ref=smat.at[e, s, :, stripe(me)],
            send_sem=rs.at[e, s, k],
            recv_sem=rr.at[e, s, k],
            device_id={"energy": p},
            device_id_type=MESH,
        )

    def keep(e, s):
        return pltpu.make_async_copy(
            sig.at[s, :, 2 * me + e], smat.at[e, s, :, stripe(me)], rr.at[e, s, 0]
        )

    def send_back(e, s):
        for k in range(1, PEERS):
            giveback(e, s, k).start()
        keep(e, s).start()

    def row_products(e):
        for i in range(2):
            for k in range(1, SIDE):
                send_m(e, k, i).wait_recv()
        eye = (
            lax.broadcasted_iota(jnp.int32, (NORB, NORB), 0)
            == lax.broadcasted_iota(jnp.int32, (NORB, NORB), 1)
        )
        zh[0, 0] = jnp.zeros((NORB, NORB), BF16)
        zh[0, 1] = jnp.where(eye, 1.0, 0.0).astype(BF16)
        zh[0, 2] = jnp.zeros((NORB, NORB), BF16)
        zl[0] = jnp.zeros((3, NORB, NORB), BF16)

        @pl.loop(0, SIDE)
        def _(j):
            now = j % 2

            @pl.when(j == z)
            def _():
                yh[e] = zh[now]
                yl[e] = zl[now]

            mh[j, e, 0] = -mh[j, e, 2]
            ml[j, e, 0] = -ml[j, e, 2]
            value = product(mh[j, e], ml[j, e], rows(zh[now, 1:3]), rows(zl[now, 1:3]))
            high, low = split(value)
            put3(zh.at[1 - now], high)
            put3(zl.at[1 - now], low)

        nh[x, e] = zh[0]
        nl[x, e] = zl[0]

        @pl.when(x > 0)
        def _():
            for i in range(2):
                upward(lambda k: send_n(e, k, i).start())

        @pl.when(x < SIDE - 1)
        def _():
            wh[e, SIDE - 2] = mh[SIDE - 1, e]
            wl[e, SIDE - 2] = ml[SIDE - 1, e]

            @pl.loop(1, SIDE - 1)
            def _(i):
                j = SIDE - 2 - i
                value = product(
                    wh[e, j + 1], wl[e, j + 1], rows(mh[j + 1, e, 1:3]), rows(ml[j + 1, e, 1:3])
                )
                high, low = split(value)
                put3(wh.at[e, j], high)
                put3(wl.at[e, j], low)

    @pl.loop(0, SLABS - 2)
    def _(s):
        convolve(s)
        send_back(0, s)

    row_products(0)

    @pl.loop(SLABS - 2, SLABS)
    def _(s):
        convolve(s)
        send_back(0, s)

    @pl.loop(0, SLABS)
    def _(s):
        send_back(1, s)

    row_products(1)

    @pl.loop(0, EN)
    def _(e):
        @pl.loop(0, SLABS)
        def _(s):
            keep(e, s).wait()
            for k in range(1, PEERS):
                giveback(e, s, k).wait_recv()
            mixed = left(g3[e, s], smat[e, s, 0], smat[e, s, 1]).astype(BF16)
            put3(ih, mixed)
            bst[e, s] = right(ih, g3[e, s]).reshape(2, NORB, NORB)

            @pl.when(s > 0)
            def _():
                value = congruence(kh[e, s], kl[e, s], rows(bst[e, s - 1]), ih, il)
                bst[e, s] += value.reshape(2, NORB, NORB)

        arow[z, e] = bst[e, SLABS - 1].astype(BF16)
        for k in (2, 1, 3):
            send_a(e, k).start()

    @pl.loop(0, EN)
    def _(e):
        pre[SIDE] = jnp.zeros((2, NORB, NORB), F32)

        @pl.loop(0, SIDE)
        def _(t):
            k = jnp.where(t < 2, t, SIDE + 1 - t)
            j = (z - k + SIDE) % SIDE

            @pl.when(k > 0)
            def _():
                send_a(e, k).wait_recv()

            @pl.when((x < SIDE - 1) & (j < SIDE - 1))
            def _():
                value = congruence(wh[e, j], wl[e, j], rows(arow[j, e]), ih, il, True)
                pre[SIDE] += value.reshape(2, NORB, NORB)

            @pl.when(j == SIDE - 1)
            def _():
                pre[SIDE] += arow[j, e].astype(F32)

        @pl.when(x < SIDE - 1)
        def _():
            rrow[x, e] = pre[SIDE].astype(BF16)
            for k in range(SIDE - 1, 0, -1):

                @pl.when(x + k < SIDE)
                def _(k=k):
                    send_r(e, k).start()

        pre[0] = jnp.zeros((2, NORB, NORB), F32)
        pre[1] = arow[0, e].astype(F32)

        @pl.loop(1, z)
        def _(j):
            value = congruence(mh[j, e], ml[j, e], rows(pre[j]), ih, il)
            pre[j + 1] = value.reshape(2, NORB, NORB) + arow[j, e].astype(F32)

        cin[e] = pre[z]

    def store(e, s):
        return pltpu.make_async_copy(bst.at[e, s], out_hbm.at[:, e, s], od.at[e, s])

    @pl.loop(0, EN)
    def _(e):
        def step(j, exact):
            for i in range(2):
                send_n(e, x - j, i).wait_recv()
            nh[j, e, 0] = -nh[j, e, 2]
            nl[j, e, 0] = -nl[j, e, 2]
            value = congruence(nh[j, e], nl[j, e], rows(pre[j]), ih, il, exact)
            pre[j + 1] = value.reshape(2, NORB, NORB)
            send_r(e, x - j).wait_recv()
            pre[j + 1] += rrow[j, e].astype(F32)

        @pl.when(x > 0)
        def _():
            send_r(e, x).wait_recv()
            pre[1] = rrow[0, e].astype(F32)

            @pl.when(x > 1)
            def _():
                step(1, True)

                @pl.loop(2, x)
                def _(j):
                    step(j, False)

            value = congruence(yh[e], yl[e], rows(pre[x]), ih, il)
            cin[e] += value.reshape(2, NORB, NORB)

        @pl.loop(0, SLABS)
        def _(s):
            @pl.when(slab > 0)
            def _():
                value = congruence(ph[e, s], pw[e, s], rows(cin[e]), ih, il, True, True)
                bst[e, s] += value.reshape(2, NORB, NORB)

            store(e, s).start()

    for e in range(EN):
        for s in range(SLABS):
            store(e, s).wait()
        for k in range(1, SIDE):
            send_m(e, k, 0).wait_send()
            send_m(e, k, 1).wait_send()
            send_a(e, k).wait_send()
        upward(lambda k: send_r(e, k).wait_send())

        @pl.when(x > 0)
        def _(e=e):
            for i in range(2):
                upward(lambda k: send_n(e, k, i).wait_send())

        for s in range(SLABS):
            for k in range(1, PEERS):
                giveback(e, s, k).wait_send()
    for s in range(SLABS):
        for k in range(1, PEERS):
            for a in range(2):
                forward(a, s, k).wait_send()


def per_device(green_lesser, screened_lesser, green_retarded, coupling):
    block = (NORB, NORB)
    dma = pltpu.SemaphoreType.DMA
    return pl.pallas_call(
        kernel,
        out_shape=jax.ShapeDtypeStruct((2, EN, SLABS) + block, F32),
        in_specs=[pl.BlockSpec(memory_space=pl.ANY)] * 4,
        out_specs=pl.BlockSpec(memory_space=pl.ANY),
        scratch_shapes=[
            pltpu.VMEM((SLABS, 2, POINTS, STRIPE, NORB), BF16),
            pltpu.VMEM((SLABS, 2, POINTS, STRIPE, NORB), BF16),
            pltpu.VMEM((SLABS, 2, POINTS, STRIPE, NORB), BF16),
            pltpu.VMEM((EN, SLABS, 2) + block, BF16),
            pltpu.VMEM((EN, SLABS, 3) + block, BF16),
            pltpu.VMEM((2, SLABS) + block, BF16),
            pltpu.VMEM((EN, SLABS, 3) + block, BF16),
            pltpu.VMEM((EN, SLABS, 3) + block, BF16),
            pltpu.VMEM((EN, SLABS, 3) + block, BF16),
            pltpu.VMEM((EN, SLABS, 3) + block, BF16),
            pltpu.VMEM((EN, 3) + block, BF16),
            pltpu.VMEM((EN, 3) + block, BF16),
            pltpu.VMEM((EN, SIDE - 1, 3) + block, BF16),
            pltpu.VMEM((EN, SIDE - 1, 3) + block, BF16),
            pltpu.VMEM((EN, SLABS, 2) + block, F32),
            pltpu.VMEM((EN, 2) + block, F32),
            pltpu.VMEM((SIDE, EN, 3) + block, BF16),
            pltpu.VMEM((SIDE, EN, 3) + block, BF16),
            pltpu.VMEM((SIDE, EN, 3) + block, BF16),
            pltpu.VMEM((SIDE, EN, 3) + block, BF16),
            pltpu.VMEM((SIDE, EN, 2) + block, BF16),
            pltpu.VMEM((SIDE, EN, 2) + block, BF16),
            pltpu.VMEM((2, 3) + block, BF16),
            pltpu.VMEM((2, 3) + block, BF16),
            pltpu.VMEM((SIDE + 1, 2) + block, F32),
            pltpu.VMEM((3,) + block, BF16),
            pltpu.VMEM((3,) + block, BF16),
            pltpu.VMEM((2, POINTS, 16, 128), F32),
            pltpu.VMEM((2, POINTS, 16, 128), F32),
            dma((2, SLABS, PEERS)),
            dma((2, SLABS, PEERS)),
            dma((EN, SLABS, PEERS)),
            dma((EN, SLABS, PEERS)),
            dma((2, EN, SIDE)),
            dma((2, EN, SIDE)),
            dma((2, EN, SIDE)),
            dma((2, EN, SIDE)),
            dma((EN, SIDE)),
            dma((EN, SIDE)),
            dma((EN, SIDE)),
            dma((EN, SIDE)),
            dma((EN, SLABS + 1)),
            dma((EN, SLABS)),
        ],
        compiler_params=pltpu.CompilerParams(
            collective_id=0, has_side_effects=True, vmem_limit_bytes=63000 * 1024
        ),
        name="born_step",
    )(green_lesser, screened_lesser, green_retarded, coupling)


def solution(mesh):
    placed = (
        P(None, "energy", "slab", None, None),
        P(None, "energy", "slab", None, None),
        P(None, "energy", "slab", None, None),
        P(None, "slab", None, None),
    )
    return jax.shard_map(
        per_device,
        mesh=mesh,
        in_specs=placed,
        out_specs=P(None, "energy", "slab", None, None),
        check_vma=False,
    )
```

```python
import jax
import jax.numpy as jnp
from jax import lax
from jax.experimental import pallas as pl
from jax.experimental.pallas import tpu as pltpu
from jax.sharding import PartitionSpec as P

F32 = jnp.float32
BF16 = jnp.bfloat16
NORB = 256
POINTS = 16
MIDDLE = POINTS // 2
PEERS = 8
STRIPE = NORB // PEERS
SLABS = 4
EN = 2
SIDE = 4
MESH = pl.DeviceIdType.MESH


def nn(a, b):
    return lax.dot_general(a, b, (((1,), (0,)), ((), ())), preferred_element_type=F32)


def nt(a, b):
    return lax.dot_general(a, b, (((1,), (1,)), ((), ())), preferred_element_type=F32)


def rows(pair):
    return pair.reshape(2 * NORB, NORB)


def left(x3, re, im):
    return nn(rows(x3[1:3]), re) + nn(rows(x3[0:2]), im)


def right(i3, x3):
    return nt(rows(i3[1:3]), x3[1]) + nt(rows(i3[0:2]), x3[0])


def split(value):
    high = value.astype(BF16)
    low = (value - high.astype(F32)).astype(BF16)
    return high, low


def put3(ref, pair):
    ref[1:3] = pair.reshape(2, NORB, NORB)
    ref[0] = -pair[NORB:]


def product(xh, xl, ch, cl):
    total = left(xh, ch[:NORB], ch[NORB:]) + left(xl, ch[:NORB], ch[NORB:])
    if cl is not None:
        total = total + left(xh, cl[:NORB], cl[NORB:])
    return total


def congruence(xh, xl, state, ih, il, exact=False, brief=False):
    high, low = (state.astype(BF16), None) if exact else split(state)
    inner = product(xh, xl, high, low)
    if brief:
        put3(ih, inner.astype(BF16))
        return right(ih, xh) + right(ih, xl)
    high, low = split(inner)
    put3(ih, high)
    put3(il, low)
    return right(ih, xh) + right(il, xh) + right(ih, xl)


def kernel(
    g_hbm, w_hbm, r_hbm, t_hbm, out_hbm,
    gbuf, wbuf, sig, smat, g3, coup, kh, kl, ph, pw, vh, vl, wh, wl, bst, cin,
    mh, ml, nh, nl, arow, rrow, zh, zl, pre, ih, il, gf, wf,
    fs, fr, rs, rr, ms, mr, ns, nr, asend, arecv, xs, xr, ld, od,
):
    slab = lax.axis_index("slab")
    me = lax.axis_index("energy")
    x = slab // SIDE
    z = slab % SIDE

    def energy_peer(k):
        return {"energy": (me + k) % PEERS}

    def z_peer(k):
        return {"slab": x * SIDE + (z + k) % SIDE}

    def x_peer(k):
        return {"slab": ((x + k) % SIDE) * SIDE + z}

    barrier = pltpu.get_barrier_semaphore()
    for k in range(1, PEERS):
        pl.semaphore_signal(barrier, inc=1, device_id=energy_peer(k), device_id_type=MESH)
    for k in range(1, SIDE):
        pl.semaphore_signal(barrier, inc=1, device_id=z_peer(k), device_id_type=MESH)
        pl.semaphore_signal(barrier, inc=1, device_id=x_peer(k), device_id_type=MESH)

    loads = []
    for e in range(EN):
        for s in range(SLABS):
            cp = pltpu.make_async_copy(r_hbm.at[:, e, s], g3.at[e, s, pl.ds(1, 2)], ld.at[e, s])
            cp.start()
            loads.append(cp)
    cp = pltpu.make_async_copy(t_hbm, coup, ld.at[0, SLABS])
    cp.start()
    loads.append(cp)

    def stripe(p):
        return pl.ds(pl.multiple_of(p * STRIPE, STRIPE), STRIPE)

    own = pl.ds(2 * me, EN)
    arrays = ((g_hbm, gbuf), (w_hbm, wbuf))

    def local_stripe(a, s):
        return pltpu.make_async_copy(
            arrays[a][0].at[:, :, s, stripe(me)], arrays[a][1].at[s, :, own], fr.at[a, s, 0]
        )

    def forward(a, s, k):
        p = (me + k) % PEERS
        return pltpu.make_async_remote_copy(
            src_ref=arrays[a][0].at[:, :, s, stripe(p)],
            dst_ref=arrays[a][1].at[s, :, own],
            send_sem=fs.at[a, s, k],
            recv_sem=fr.at[a, s, k],
            device_id={"energy": p},
            device_id_type=MESH,
        )

    pl.semaphore_wait(barrier, PEERS - 1 + 2 * (SIDE - 1))
    for s in range(SLABS):
        for k in range(1, PEERS):
            for a in range(2):
                forward(a, s, k).start()
        for a in range(2):
            local_stripe(a, s).start()

    def gather(k, source, target, send, recv, peer):
        return pltpu.make_async_remote_copy(
            src_ref=source, dst_ref=target, send_sem=send, recv_sem=recv,
            device_id=peer, device_id_type=MESH,
        )

    def send_m(e, k, i):
        view = (mh, ml)[i].at[z, e, pl.ds(1, 2)]
        return gather(k, view, view, ms.at[i, e, k], mr.at[i, e, k], z_peer(k))

    def send_n(e, k, i):
        view = (nh, nl)[i].at[x - 1, e]
        return gather(k, view, view, ns.at[i, e, k], nr.at[i, e, k], x_peer(k))

    def upward(act):
        for k in range(1, SIDE):
            pl.when(x + k < SIDE)(lambda k=k: act(k))

    def send_a(e, k):
        view = arow.at[z, e]
        return gather(k, view, view, asend.at[e, k], arecv.at[e, k], z_peer(k))

    def send_r(e, k):
        view = rrow.at[x, e]
        return gather(k, view, view, xs.at[e, k], xr.at[e, k], x_peer(k))

    for cp in loads:
        cp.wait()

    @pl.loop(0, EN)
    def _(e):
        @pl.loop(0, SLABS)
        def _(s):
            g3[e, s, 0] = -g3[e, s, 2]
            high, low = split(left(g3[e, s], coup[0, s], coup[1, s]))
            put3(kh.at[e, s], high)
            put3(kl.at[e, s], low)

        ph[e, 0] = kh[e, 0]
        pw[e, 0] = kl[e, 0]

        @pl.loop(1, SLABS)
        def _(s):
            value = product(kh[e, s], kl[e, s], rows(ph[e, s - 1, 1:3]), rows(pw[e, s - 1, 1:3]))
            high, low = split(value)
            put3(ph.at[e, s], high)
            put3(pw.at[e, s], low)

        mh[z, e] = ph[e, SLABS - 1]
        ml[z, e] = pw[e, SLABS - 1]
        for i in range(2):
            for k in range(1, SIDE):
                send_m(e, k, i).start()

    def convolve(s):
        for a in range(2):
            local_stripe(a, s).wait()
        for k in range(1, PEERS):
            for a in range(2):
                forward(a, s, k).wait_recv()

        @pl.loop(0, STRIPE // 16)
        def _(tr):
            @pl.loop(0, NORB // 128)
            def _(tc):
                rr_ = pl.ds(pl.multiple_of(tr * 16, 16), 16)
                cc_ = pl.ds(pl.multiple_of(tc * 128, 128), 128)
                for part in range(2):
                    for m in range(POINTS):
                        gf[part, m] = gbuf[s, part, m, rr_, cc_].astype(F32)
                        wf[part, m] = wbuf[s, part, m, rr_, cc_].astype(F32)
                for n in range(POINTS):
                    re = None
                    im = None
                    for m in range(max(0, n + MIDDLE + 1 - POINTS), min(POINTS, n + MIDDLE + 1)):
                        l = n - m + MIDDLE
                        a, b = gf[0, m], gf[1, m]
                        c, d = wf[0, l], wf[1, l]
                        r = a * c - b * d
                        i = a * d + b * c
                        re = r if re is None else re + r
                        im = i if im is None else im + i
                    sig[s, 0, n, rr_, cc_] = (im * (-1.0 / POINTS)).astype(BF16)
                    sig[s, 1, n, rr_, cc_] = (re * (1.0 / POINTS)).astype(BF16)

    def giveback(e, s, k):
        p = (me + k) % PEERS
        return pltpu.make_async_remote_copy(
            src_ref=sig.at[s, :, 2 * p + e],
            dst_ref=smat.at[e, s, :, stripe(me)],
            send_sem=rs.at[e, s, k],
            recv_sem=rr.at[e, s, k],
            device_id={"energy": p},
            device_id_type=MESH,
        )

    def keep(e, s):
        return pltpu.make_async_copy(
            sig.at[s, :, 2 * me + e], smat.at[e, s, :, stripe(me)], rr.at[e, s, 0]
        )

    def send_back(e, s):
        for k in range(1, PEERS):
            giveback(e, s, k).start()
        keep(e, s).start()

    def row_products(e):
        for i in range(2):
            for k in range(1, SIDE):
                send_m(e, k, i).wait_recv()
        eye = (
            lax.broadcasted_iota(jnp.int32, (NORB, NORB), 0)
            == lax.broadcasted_iota(jnp.int32, (NORB, NORB), 1)
        )
        zh[0, 0] = jnp.zeros((NORB, NORB), BF16)
        zh[0, 1] = jnp.where(eye, 1.0, 0.0).astype(BF16)
        zh[0, 2] = jnp.zeros((NORB, NORB), BF16)
        zl[0] = jnp.zeros((3, NORB, NORB), BF16)

        @pl.loop(0, SIDE)
        def _(j):
            now = j % 2

            @pl.when(j == z)
            def _():
                first = jnp.maximum(x - 1, 0)
                vh[e, first] = zh[now]
                vl[e, first] = zl[now]

            mh[j, e, 0] = -mh[j, e, 2]
            ml[j, e, 0] = -ml[j, e, 2]
            value = product(mh[j, e], ml[j, e], rows(zh[now, 1:3]), rows(zl[now, 1:3]))
            high, low = split(value)
            put3(zh.at[1 - now], high)
            put3(zl.at[1 - now], low)

        @pl.when((x > 0) & (x < SIDE - 1))
        def _():
            nh[x - 1, e] = zh[0, 1:3]
            nl[x - 1, e] = zl[0, 1:3]
            for i in range(2):
                upward(lambda k: send_n(e, k, i).start())

        @pl.when(x < SIDE - 1)
        def _():
            wh[e, SIDE - 2] = mh[SIDE - 1, e]
            wl[e, SIDE - 2] = ml[SIDE - 1, e]

            @pl.loop(1, SIDE - 1)
            def _(i):
                j = SIDE - 2 - i
                value = product(
                    wh[e, j + 1], wl[e, j + 1], rows(mh[j + 1, e, 1:3]), rows(ml[j + 1, e, 1:3])
                )
                high, low = split(value)
                put3(wh.at[e, j], high)
                put3(wl.at[e, j], low)

    @pl.loop(0, SLABS - 2)
    def _(s):
        convolve(s)
        send_back(0, s)

    row_products(0)

    @pl.loop(SLABS - 2, SLABS)
    def _(s):
        convolve(s)
        send_back(0, s)

    @pl.loop(0, SLABS)
    def _(s):
        send_back(1, s)

    row_products(1)

    @pl.loop(0, EN)
    def _(e):
        @pl.loop(0, SLABS)
        def _(s):
            keep(e, s).wait()
            for k in range(1, PEERS):
                giveback(e, s, k).wait_recv()
            mixed = left(g3[e, s], smat[e, s, 0], smat[e, s, 1]).astype(BF16)
            put3(ih, mixed)
            bst[e, s] = right(ih, g3[e, s]).reshape(2, NORB, NORB)

            @pl.when(s > 0)
            def _():
                value = congruence(kh[e, s], kl[e, s], rows(bst[e, s - 1]), ih, il)
                bst[e, s] += value.reshape(2, NORB, NORB)

        arow[z, e] = bst[e, SLABS - 1].astype(BF16)
        for k in (2, 1, 3):
            send_a(e, k).start()

    @pl.loop(0, EN)
    def _(e):
        @pl.loop(1, x)
        def _(i):
            j = x - i
            for part in range(2):
                pltpu.make_async_copy(
                    (nh, nl)[part].at[j - 1, e], (nh, nl)[part].at[j - 1, e], nr.at[part, e, x - j]
                ).wait()
            value = product(vh[e, j], vl[e, j], rows(nh[j - 1, e]), rows(nl[j - 1, e]))
            high, low = split(value)
            put3(vh.at[e, j - 1], high)
            put3(vl.at[e, j - 1], low)

        pre[SIDE] = jnp.zeros((2, NORB, NORB), F32)

        @pl.loop(0, SIDE)
        def _(t):
            k = jnp.where(t < 2, t, SIDE + 1 - t)
            j = (z - k + SIDE) % SIDE

            @pl.when(k > 0)
            def _():
                send_a(e, k).wait_recv()

            @pl.when((x < SIDE - 1) & (j < SIDE - 1))
            def _():
                value = congruence(wh[e, j], wl[e, j], rows(arow[j, e]), ih, il, True)
                pre[SIDE] += value.reshape(2, NORB, NORB)

            @pl.when(j == SIDE - 1)
            def _():
                pre[SIDE] += arow[j, e].astype(F32)

        @pl.when(x < SIDE - 1)
        def _():
            rrow[x, e] = pre[SIDE].astype(BF16)
            for k in range(SIDE - 1, 0, -1):

                @pl.when(x + k < SIDE)
                def _(k=k):
                    send_r(e, k).start()

        pre[0] = jnp.zeros((2, NORB, NORB), F32)
        pre[1] = arow[0, e].astype(F32)

        @pl.loop(1, z)
        def _(j):
            value = congruence(mh[j, e], ml[j, e], rows(pre[j]), ih, il)
            pre[j + 1] = value.reshape(2, NORB, NORB) + arow[j, e].astype(F32)

        cin[e] = pre[z]

    def store(e, s):
        return pltpu.make_async_copy(bst.at[e, s], out_hbm.at[:, e, s], od.at[e, s])

    @pl.loop(0, EN)
    def _(e):
        @pl.loop(0, x)
        def _(t):
            k = jnp.where(x < SIDE - 1, t + 1, jnp.where(t == 0, SIDE - 1, t))
            j = x - k
            send_r(e, k).wait_recv()
            value = congruence(vh[e, j], vl[e, j], rows(rrow[j, e]), ih, il, True)
            cin[e] += value.reshape(2, NORB, NORB)

        @pl.loop(0, SLABS)
        def _(s):
            @pl.when(slab == 0)
            def _():
                bst[e, s] = bst[e, s] * 0.5

            @pl.when(slab > 0)
            def _():
                value = congruence(ph[e, s], pw[e, s], rows(cin[e]), ih, il, True, True)
                bst[e, s] = (bst[e, s] + value.reshape(2, NORB, NORB)) * 0.5

            store(e, s).start()

    for e in range(EN):
        for s in range(SLABS):
            store(e, s).wait()
        for k in range(1, SIDE):
            send_m(e, k, 0).wait_send()
            send_m(e, k, 1).wait_send()
            send_a(e, k).wait_send()
        upward(lambda k: send_r(e, k).wait_send())

        @pl.when((x > 0) & (x < SIDE - 1))
        def _(e=e):
            for i in range(2):
                upward(lambda k: send_n(e, k, i).wait_send())

        for s in range(SLABS):
            for k in range(1, PEERS):
                giveback(e, s, k).wait_send()
    for s in range(SLABS):
        for k in range(1, PEERS):
            for a in range(2):
                forward(a, s, k).wait_send()


def per_device(green_lesser, screened_lesser, green_retarded, coupling):
    block = (NORB, NORB)
    dma = pltpu.SemaphoreType.DMA
    half = pl.pallas_call(
        kernel,
        out_shape=jax.ShapeDtypeStruct((2, EN, SLABS) + block, F32),
        in_specs=[pl.BlockSpec(memory_space=pl.ANY)] * 4,
        out_specs=pl.BlockSpec(memory_space=pl.ANY),
        scratch_shapes=[
            pltpu.VMEM((SLABS, 2, POINTS, STRIPE, NORB), BF16),
            pltpu.VMEM((SLABS, 2, POINTS, STRIPE, NORB), BF16),
            pltpu.VMEM((SLABS, 2, POINTS, STRIPE, NORB), BF16),
            pltpu.VMEM((EN, SLABS, 2) + block, BF16),
            pltpu.VMEM((EN, SLABS, 3) + block, BF16),
            pltpu.VMEM((2, SLABS) + block, BF16),
            pltpu.VMEM((EN, SLABS, 3) + block, BF16),
            pltpu.VMEM((EN, SLABS, 3) + block, BF16),
            pltpu.VMEM((EN, SLABS, 3) + block, BF16),
            pltpu.VMEM((EN, SLABS, 3) + block, BF16),
            pltpu.VMEM((EN, SIDE - 1, 3) + block, BF16),
            pltpu.VMEM((EN, SIDE - 1, 3) + block, BF16),
            pltpu.VMEM((EN, SIDE - 1, 3) + block, BF16),
            pltpu.VMEM((EN, SIDE - 1, 3) + block, BF16),
            pltpu.VMEM((EN, SLABS, 2) + block, F32),
            pltpu.VMEM((EN, 2) + block, F32),
            pltpu.VMEM((SIDE, EN, 3) + block, BF16),
            pltpu.VMEM((SIDE, EN, 3) + block, BF16),
            pltpu.VMEM((SIDE - 2, EN, 2) + block, BF16),
            pltpu.VMEM((SIDE - 2, EN, 2) + block, BF16),
            pltpu.VMEM((SIDE, EN, 2) + block, BF16),
            pltpu.VMEM((SIDE, EN, 2) + block, BF16),
            pltpu.VMEM((2, 3) + block, BF16),
            pltpu.VMEM((2, 3) + block, BF16),
            pltpu.VMEM((SIDE + 1, 2) + block, F32),
            pltpu.VMEM((3,) + block, BF16),
            pltpu.VMEM((3,) + block, BF16),
            pltpu.VMEM((2, POINTS, 16, 128), F32),
            pltpu.VMEM((2, POINTS, 16, 128), F32),
            dma((2, SLABS, PEERS)),
            dma((2, SLABS, PEERS)),
            dma((EN, SLABS, PEERS)),
            dma((EN, SLABS, PEERS)),
            dma((2, EN, SIDE)),
            dma((2, EN, SIDE)),
            dma((2, EN, SIDE)),
            dma((2, EN, SIDE)),
            dma((EN, SIDE)),
            dma((EN, SIDE)),
            dma((EN, SIDE)),
            dma((EN, SIDE)),
            dma((EN, SLABS + 1)),
            dma((EN, SLABS)),
        ],
        compiler_params=pltpu.CompilerParams(
            collective_id=0, has_side_effects=True, vmem_limit_bytes=63000 * 1024
        ),
        name="born_step",
    )(green_lesser, screened_lesser, green_retarded, coupling)
    return half * 2.0


def solution(mesh):
    placed = (
        P(None, "energy", "slab", None, None),
        P(None, "energy", "slab", None, None),
        P(None, "energy", "slab", None, None),
        P(None, "slab", None, None),
    )
    return jax.shard_map(
        per_device,
        mesh=mesh,
        in_specs=placed,
        out_specs=P(None, "energy", "slab", None, None),
        check_vma=False,
    )
```

```python
import jax
import jax.numpy as jnp
from jax import lax
from jax.experimental import pallas as pl
from jax.experimental.pallas import tpu as pltpu
from jax.sharding import PartitionSpec as P

F32 = jnp.float32
BF16 = jnp.bfloat16
NORB = 256
POINTS = 16
MIDDLE = POINTS // 2
PEERS = 8
STRIPE = NORB // PEERS
SLABS = 4
EN = 2
SIDE = 4
MESH = pl.DeviceIdType.MESH


def nn(a, b):
    return lax.dot_general(a, b, (((1,), (0,)), ((), ())), preferred_element_type=F32)


def nt(a, b):
    return lax.dot_general(a, b, (((1,), (1,)), ((), ())), preferred_element_type=F32)


def rows(pair):
    return pair.reshape(2 * NORB, NORB)


def left(x3, re, im):
    return nn(rows(x3[1:3]), re) + nn(rows(x3[0:2]), im)


def right(i3, x3):
    return nt(rows(i3[1:3]), x3[1]) + nt(rows(i3[0:2]), x3[0])


def split(value):
    high = value.astype(BF16)
    low = (value - high.astype(F32)).astype(BF16)
    return high, low


def put3(ref, pair):
    ref[1:3] = pair.reshape(2, NORB, NORB)
    ref[0] = -pair[NORB:]


def product(xh, xl, ch, cl):
    total = left(xh, ch[:NORB], ch[NORB:]) + left(xl, ch[:NORB], ch[NORB:])
    if cl is not None:
        total = total + left(xh, cl[:NORB], cl[NORB:])
    return total


def congruence(xh, xl, state, ih, il, exact=False, brief=False):
    high, low = (state.astype(BF16), None) if exact else split(state)
    inner = product(xh, xl, high, low)
    if brief:
        put3(ih, inner.astype(BF16))
        return right(ih, xh) + right(ih, xl)
    high, low = split(inner)
    put3(ih, high)
    put3(il, low)
    return right(ih, xh) + right(il, xh) + right(ih, xl)


def kernel(
    g_hbm, w_hbm, r_hbm, t_hbm, out_hbm,
    gbuf, wbuf, sig, smat, g3, coup, kh, kl, ph, pw, vh, vl, wh, wl, bst, cin,
    mh, ml, nh, nl, arow, rrow, zh, zl, pre, ih, il, gf, wf,
    fs, fr, rs, rr, ms, mr, ns, nr, asend, arecv, xs, xr, ld, od,
):
    slab = lax.axis_index("slab")
    me = lax.axis_index("energy")
    x = slab // SIDE
    z = slab % SIDE

    def energy_peer(k):
        return {"energy": (me + k) % PEERS}

    def z_peer(k):
        return {"slab": x * SIDE + (z + k) % SIDE}

    def x_peer(k):
        return {"slab": ((x + k) % SIDE) * SIDE + z}

    barrier = pltpu.get_barrier_semaphore()
    for k in range(1, PEERS):
        pl.semaphore_signal(barrier, inc=1, device_id=energy_peer(k), device_id_type=MESH)
    for k in range(1, SIDE):
        pl.semaphore_signal(barrier, inc=1, device_id=z_peer(k), device_id_type=MESH)
        pl.semaphore_signal(barrier, inc=1, device_id=x_peer(k), device_id_type=MESH)

    loads = []
    for e in range(EN):
        for s in range(SLABS):
            cp = pltpu.make_async_copy(r_hbm.at[:, e, s], g3.at[e, s, pl.ds(1, 2)], ld.at[e, s])
            cp.start()
            loads.append(cp)
    cp = pltpu.make_async_copy(t_hbm, coup, ld.at[0, SLABS])
    cp.start()
    loads.append(cp)

    def stripe(p):
        return pl.ds(pl.multiple_of(p * STRIPE, STRIPE), STRIPE)

    own = pl.ds(2 * me, EN)
    arrays = ((g_hbm, gbuf), (w_hbm, wbuf))

    def local_stripe(a, s):
        return pltpu.make_async_copy(
            arrays[a][0].at[:, :, s, stripe(me)], arrays[a][1].at[s, :, own], fr.at[a, s, 0]
        )

    def forward(a, s, k):
        p = (me + k) % PEERS
        return pltpu.make_async_remote_copy(
            src_ref=arrays[a][0].at[:, :, s, stripe(p)],
            dst_ref=arrays[a][1].at[s, :, own],
            send_sem=fs.at[a, s, k],
            recv_sem=fr.at[a, s, k],
            device_id={"energy": p},
            device_id_type=MESH,
        )

    pl.semaphore_wait(barrier, PEERS - 1 + 2 * (SIDE - 1))
    for s in range(SLABS):
        for k in range(1, PEERS):
            for a in range(2):
                forward(a, s, k).start()
        for a in range(2):
            local_stripe(a, s).start()

    def gather(k, source, target, send, recv, peer):
        return pltpu.make_async_remote_copy(
            src_ref=source, dst_ref=target, send_sem=send, recv_sem=recv,
            device_id=peer, device_id_type=MESH,
        )

    def send_m(e, k, i):
        view = (mh, ml)[i].at[z, e, pl.ds(1, 2)]
        return gather(k, view, view, ms.at[i, e, k], mr.at[i, e, k], z_peer(k))

    def send_n(e, k, i):
        view = (nh, nl)[i].at[x - 1, e]
        return gather(k, view, view, ns.at[i, e, k], nr.at[i, e, k], x_peer(k))

    def upward(act):
        for k in range(1, SIDE):
            pl.when(x + k < SIDE)(lambda k=k: act(k))

    def send_a(e, k):
        view = arow.at[z, e]
        return gather(k, view, view, asend.at[e, k], arecv.at[e, k], z_peer(k))

    def send_r(e, k):
        view = rrow.at[x, e]
        return gather(k, view, view, xs.at[e, k], xr.at[e, k], x_peer(k))

    for cp in loads:
        cp.wait()

    @pl.loop(0, EN)
    def _(e):
        @pl.loop(0, SLABS)
        def _(s):
            g3[e, s, 0] = -g3[e, s, 2]
            high, low = split(left(g3[e, s], coup[0, s], coup[1, s]))
            put3(kh.at[e, s], high)
            put3(kl.at[e, s], low)

        ph[e, 0] = kh[e, 0]
        pw[e, 0] = kl[e, 0]

        @pl.loop(1, SLABS)
        def _(s):
            value = product(kh[e, s], kl[e, s], rows(ph[e, s - 1, 1:3]), rows(pw[e, s - 1, 1:3]))
            high, low = split(value)
            put3(ph.at[e, s], high)
            put3(pw.at[e, s], low)

        mh[z, e] = ph[e, SLABS - 1]
        ml[z, e] = pw[e, SLABS - 1]
        for i in range(2):
            for k in range(1, SIDE):
                send_m(e, k, i).start()

    def convolve(s):
        for a in range(2):
            local_stripe(a, s).wait()
        for k in range(1, PEERS):
            for a in range(2):
                forward(a, s, k).wait_recv()

        @pl.loop(0, STRIPE // 16)
        def _(tr):
            @pl.loop(0, NORB // 128)
            def _(tc):
                rr_ = pl.ds(pl.multiple_of(tr * 16, 16), 16)
                cc_ = pl.ds(pl.multiple_of(tc * 128, 128), 128)
                for part in range(2):
                    for m in range(POINTS):
                        gf[part, m] = gbuf[s, part, m, rr_, cc_].astype(F32)
                        wf[part, m] = wbuf[s, part, m, rr_, cc_].astype(F32)
                for n in range(POINTS):
                    re = None
                    im = None
                    for m in range(max(0, n + MIDDLE + 1 - POINTS), min(POINTS, n + MIDDLE + 1)):
                        l = n - m + MIDDLE
                        a, b = gf[0, m], gf[1, m]
                        c, d = wf[0, l], wf[1, l]
                        r = a * c - b * d
                        i = a * d + b * c
                        re = r if re is None else re + r
                        im = i if im is None else im + i
                    sig[s, 0, n, rr_, cc_] = (im * (-1.0 / POINTS)).astype(BF16)
                    sig[s, 1, n, rr_, cc_] = (re * (1.0 / POINTS)).astype(BF16)

    def giveback(e, s, k):
        p = (me + k) % PEERS
        return pltpu.make_async_remote_copy(
            src_ref=sig.at[s, :, 2 * p + e],
            dst_ref=smat.at[e, s, :, stripe(me)],
            send_sem=rs.at[e, s, k],
            recv_sem=rr.at[e, s, k],
            device_id={"energy": p},
            device_id_type=MESH,
        )

    def keep(e, s):
        return pltpu.make_async_copy(
            sig.at[s, :, 2 * me + e], smat.at[e, s, :, stripe(me)], rr.at[e, s, 0]
        )

    def send_back(e, s, core):
        for d in (2, 1, 3, 0):
            p = ((me // 2 + d) % SIDE) * 2 + core
            k = (p - me + PEERS) % PEERS

            @pl.when(k > 0)
            def _(k=k):
                giveback(e, s, k).start()

    def row_products(e):
        for i in range(2):
            for k in range(1, SIDE):
                send_m(e, k, i).wait_recv()
        eye = (
            lax.broadcasted_iota(jnp.int32, (NORB, NORB), 0)
            == lax.broadcasted_iota(jnp.int32, (NORB, NORB), 1)
        )
        zh[0, 0] = jnp.zeros((NORB, NORB), BF16)
        zh[0, 1] = jnp.where(eye, 1.0, 0.0).astype(BF16)
        zh[0, 2] = jnp.zeros((NORB, NORB), BF16)
        zl[0] = jnp.zeros((3, NORB, NORB), BF16)

        @pl.loop(0, SIDE)
        def _(j):
            now = j % 2

            @pl.when(j == z)
            def _():
                first = jnp.maximum(x - 1, 0)
                vh[e, first] = zh[now]
                vl[e, first] = zl[now]

            mh[j, e, 0] = -mh[j, e, 2]
            ml[j, e, 0] = -ml[j, e, 2]
            value = product(mh[j, e], ml[j, e], rows(zh[now, 1:3]), rows(zl[now, 1:3]))
            high, low = split(value)
            put3(zh.at[1 - now], high)
            put3(zl.at[1 - now], low)

        @pl.when((x > 0) & (x < SIDE - 1))
        def _():
            nh[x - 1, e] = zh[0, 1:3]
            nl[x - 1, e] = zl[0, 1:3]
            for i in range(2):
                upward(lambda k: send_n(e, k, i).start())

        @pl.when(x < SIDE - 1)
        def _():
            wh[e, SIDE - 2] = mh[SIDE - 1, e]
            wl[e, SIDE - 2] = ml[SIDE - 1, e]

            @pl.loop(1, SIDE - 1)
            def _(i):
                j = SIDE - 2 - i
                value = product(
                    wh[e, j + 1], wl[e, j + 1], rows(mh[j + 1, e, 1:3]), rows(ml[j + 1, e, 1:3])
                )
                high, low = split(value)
                put3(wh.at[e, j], high)
                put3(wl.at[e, j], low)

    @pl.loop(0, SLABS - 2)
    def _(s):
        convolve(s)
        send_back(0, s, 0)
        for e in range(EN):
            keep(e, s).start()

    row_products(0)

    @pl.loop(SLABS - 2, SLABS)
    def _(s):
        convolve(s)
        send_back(0, s, 0)
        for e in range(EN):
            keep(e, s).start()

    for e, core in ((0, 1), (1, 0), (1, 1)):

        @pl.loop(0, SLABS)
        def _(s, e=e, core=core):
            send_back(e, s, core)

    row_products(1)

    def row_windows(e):
        @pl.loop(1, x)
        def _(i):
            j = x - i
            for part in range(2):
                pltpu.make_async_copy(
                    (nh, nl)[part].at[j - 1, e], (nh, nl)[part].at[j - 1, e], nr.at[part, e, x - j]
                ).wait()
            value = product(vh[e, j], vl[e, j], rows(nh[j - 1, e]), rows(nl[j - 1, e]))
            high, low = split(value)
            put3(vh.at[e, j - 1], high)
            put3(vl.at[e, j - 1], low)

    row_windows(0)

    @pl.loop(0, EN)
    def _(e):
        @pl.loop(0, SLABS)
        def _(s):
            keep(e, s).wait()
            for k in range(1, PEERS):
                giveback(e, s, k).wait_recv()
            mixed = left(g3[e, s], smat[e, s, 0], smat[e, s, 1]).astype(BF16)
            put3(ih, mixed)
            bst[e, s] = right(ih, g3[e, s]).reshape(2, NORB, NORB)

            @pl.when(s > 0)
            def _():
                value = congruence(kh[e, s], kl[e, s], rows(bst[e, s - 1]), ih, il)
                bst[e, s] += value.reshape(2, NORB, NORB)

        arow[z, e] = bst[e, SLABS - 1].astype(BF16)
        for k in (2, 1, 3):
            send_a(e, k).start()

    @pl.loop(0, EN)
    def _(e):
        @pl.when(e == 1)
        def _():
            row_windows(1)

        pre[SIDE] = jnp.zeros((2, NORB, NORB), F32)

        @pl.loop(0, SIDE)
        def _(t):
            k = jnp.where(t < 2, t, SIDE + 1 - t)
            j = (z - k + SIDE) % SIDE

            @pl.when(k > 0)
            def _():
                send_a(e, k).wait_recv()

            @pl.when((x < SIDE - 1) & (j < SIDE - 1))
            def _():
                value = congruence(wh[e, j], wl[e, j], rows(arow[j, e]), ih, il, True)
                pre[SIDE] += value.reshape(2, NORB, NORB)

            @pl.when(j == SIDE - 1)
            def _():
                pre[SIDE] += arow[j, e].astype(F32)

        @pl.when(x < SIDE - 1)
        def _():
            rrow[x, e] = pre[SIDE].astype(BF16)
            for k in range(SIDE - 1, 0, -1):

                @pl.when(x + k < SIDE)
                def _(k=k):
                    send_r(e, k).start()

        pre[0] = jnp.zeros((2, NORB, NORB), F32)
        pre[1] = arow[0, e].astype(F32)

        @pl.loop(1, z)
        def _(j):
            value = congruence(mh[j, e], ml[j, e], rows(pre[j]), ih, il)
            pre[j + 1] = value.reshape(2, NORB, NORB) + arow[j, e].astype(F32)

        cin[e] = pre[z]

    def store(e, s):
        return pltpu.make_async_copy(bst.at[e, s], out_hbm.at[:, e, s], od.at[e, s])

    @pl.loop(0, EN)
    def _(e):
        @pl.loop(0, x)
        def _(t):
            k = jnp.where(x < SIDE - 1, t + 1, jnp.where(t == 0, SIDE - 1, t))
            j = x - k
            send_r(e, k).wait_recv()
            value = congruence(vh[e, j], vl[e, j], rows(rrow[j, e]), ih, il, True)
            cin[e] += value.reshape(2, NORB, NORB)

        @pl.loop(0, SLABS)
        def _(s):
            @pl.when(slab == 0)
            def _():
                bst[e, s] = bst[e, s] * 0.5

            @pl.when(slab > 0)
            def _():
                value = congruence(ph[e, s], pw[e, s], rows(cin[e]), ih, il, True, True)
                bst[e, s] = (bst[e, s] + value.reshape(2, NORB, NORB)) * 0.5

            store(e, s).start()

    for e in range(EN):
        for s in range(SLABS):
            store(e, s).wait()
        for k in range(1, SIDE):
            send_m(e, k, 0).wait_send()
            send_m(e, k, 1).wait_send()
            send_a(e, k).wait_send()
        upward(lambda k: send_r(e, k).wait_send())

        @pl.when((x > 0) & (x < SIDE - 1))
        def _(e=e):
            for i in range(2):
                upward(lambda k: send_n(e, k, i).wait_send())

        for s in range(SLABS):
            for k in range(1, PEERS):
                giveback(e, s, k).wait_send()
    for s in range(SLABS):
        for k in range(1, PEERS):
            for a in range(2):
                forward(a, s, k).wait_send()


def per_device(green_lesser, screened_lesser, green_retarded, coupling):
    block = (NORB, NORB)
    dma = pltpu.SemaphoreType.DMA
    half = pl.pallas_call(
        kernel,
        out_shape=jax.ShapeDtypeStruct((2, EN, SLABS) + block, F32),
        in_specs=[pl.BlockSpec(memory_space=pl.ANY)] * 4,
        out_specs=pl.BlockSpec(memory_space=pl.ANY),
        scratch_shapes=[
            pltpu.VMEM((SLABS, 2, POINTS, STRIPE, NORB), BF16),
            pltpu.VMEM((SLABS, 2, POINTS, STRIPE, NORB), BF16),
            pltpu.VMEM((SLABS, 2, POINTS, STRIPE, NORB), BF16),
            pltpu.VMEM((EN, SLABS, 2) + block, BF16),
            pltpu.VMEM((EN, SLABS, 3) + block, BF16),
            pltpu.VMEM((2, SLABS) + block, BF16),
            pltpu.VMEM((EN, SLABS, 3) + block, BF16),
            pltpu.VMEM((EN, SLABS, 3) + block, BF16),
            pltpu.VMEM((EN, SLABS, 3) + block, BF16),
            pltpu.VMEM((EN, SLABS, 3) + block, BF16),
            pltpu.VMEM((EN, SIDE - 1, 3) + block, BF16),
            pltpu.VMEM((EN, SIDE - 1, 3) + block, BF16),
            pltpu.VMEM((EN, SIDE - 1, 3) + block, BF16),
            pltpu.VMEM((EN, SIDE - 1, 3) + block, BF16),
            pltpu.VMEM((EN, SLABS, 2) + block, F32),
            pltpu.VMEM((EN, 2) + block, F32),
            pltpu.VMEM((SIDE, EN, 3) + block, BF16),
            pltpu.VMEM((SIDE, EN, 3) + block, BF16),
            pltpu.VMEM((SIDE - 2, EN, 2) + block, BF16),
            pltpu.VMEM((SIDE - 2, EN, 2) + block, BF16),
            pltpu.VMEM((SIDE, EN, 2) + block, BF16),
            pltpu.VMEM((SIDE, EN, 2) + block, BF16),
            pltpu.VMEM((2, 3) + block, BF16),
            pltpu.VMEM((2, 3) + block, BF16),
            pltpu.VMEM((SIDE + 1, 2) + block, F32),
            pltpu.VMEM((3,) + block, BF16),
            pltpu.VMEM((3,) + block, BF16),
            pltpu.VMEM((2, POINTS, 16, 128), F32),
            pltpu.VMEM((2, POINTS, 16, 128), F32),
            dma((2, SLABS, PEERS)),
            dma((2, SLABS, PEERS)),
            dma((EN, SLABS, PEERS)),
            dma((EN, SLABS, PEERS)),
            dma((2, EN, SIDE)),
            dma((2, EN, SIDE)),
            dma((2, EN, SIDE)),
            dma((2, EN, SIDE)),
            dma((EN, SIDE)),
            dma((EN, SIDE)),
            dma((EN, SIDE)),
            dma((EN, SIDE)),
            dma((EN, SLABS + 1)),
            dma((EN, SLABS)),
        ],
        compiler_params=pltpu.CompilerParams(
            collective_id=0, has_side_effects=True, vmem_limit_bytes=63000 * 1024
        ),
        name="born_step",
    )(green_lesser, screened_lesser, green_retarded, coupling)
    return half * 2.0


def solution(mesh):
    placed = (
        P(None, "energy", "slab", None, None),
        P(None, "energy", "slab", None, None),
        P(None, "energy", "slab", None, None),
        P(None, "slab", None, None),
    )
    return jax.shard_map(
        per_device,
        mesh=mesh,
        in_specs=placed,
        out_specs=P(None, "energy", "slab", None, None),
        check_vma=False,
    )
```

```python
import jax
import jax.numpy as jnp
from jax import lax
from jax.experimental import pallas as pl
from jax.experimental.pallas import tpu as pltpu
from jax.sharding import PartitionSpec as P

F32 = jnp.float32
BF16 = jnp.bfloat16
NORB = 256
POINTS = 16
MIDDLE = POINTS // 2
PEERS = 8
STRIPE = NORB // PEERS
SLABS = 4
EN = 2
SIDE = 4
MESH = pl.DeviceIdType.MESH


def nn(a, b):
    return lax.dot_general(a, b, (((1,), (0,)), ((), ())), preferred_element_type=F32)


def nt(a, b):
    return lax.dot_general(a, b, (((1,), (1,)), ((), ())), preferred_element_type=F32)


def rows(pair):
    return pair.reshape(2 * NORB, NORB)


def left(x3, re, im):
    return nn(rows(x3[1:3]), re) + nn(rows(x3[0:2]), im)


def right(i3, x3):
    return nt(rows(i3[1:3]), x3[1]) + nt(rows(i3[0:2]), x3[0])


def split(value):
    high = value.astype(BF16)
    low = (value - high.astype(F32)).astype(BF16)
    return high, low


def put3(ref, pair):
    ref[1:3] = pair.reshape(2, NORB, NORB)
    ref[0] = -pair[NORB:]


def product(xh, xl, ch, cl):
    total = left(xh, ch[:NORB], ch[NORB:]) + left(xl, ch[:NORB], ch[NORB:])
    if cl is not None:
        total = total + left(xh, cl[:NORB], cl[NORB:])
    return total


def congruence(xh, xl, state, ih, il, exact=False, brief=False):
    high, low = (state.astype(BF16), None) if exact else split(state)
    inner = product(xh, xl, high, low)
    if brief:
        put3(ih, inner.astype(BF16))
        return right(ih, xh) + right(ih, xl)
    high, low = split(inner)
    put3(ih, high)
    put3(il, low)
    return right(ih, xh) + right(il, xh) + right(ih, xl)


def kernel(
    g_hbm, w_hbm, r_hbm, t_hbm, out_hbm,
    gbuf, wbuf, sig, smat, g3, coup, kh, kl, ph, pw, vh, vl, wh, wl, bst, cin,
    mh, ml, nh, nl, arow, rrow, zh, zl, pre, ih, il, gf, wf,
    fs, fr, rs, rr, ms, mr, ns, nr, asend, arecv, xs, xr, ld, od,
):
    slab = lax.axis_index("slab")
    me = lax.axis_index("energy")
    x = slab // SIDE
    z = slab % SIDE

    def energy_peer(k):
        return {"energy": (me + k) % PEERS}

    def z_peer(k):
        return {"slab": x * SIDE + (z + k) % SIDE}

    def x_peer(k):
        return {"slab": ((x + k) % SIDE) * SIDE + z}

    barrier = pltpu.get_barrier_semaphore()
    for k in range(1, PEERS):
        pl.semaphore_signal(barrier, inc=1, device_id=energy_peer(k), device_id_type=MESH)
    for k in range(1, SIDE):
        pl.semaphore_signal(barrier, inc=1, device_id=z_peer(k), device_id_type=MESH)
        pl.semaphore_signal(barrier, inc=1, device_id=x_peer(k), device_id_type=MESH)

    loads = []
    for e in range(EN):
        for s in range(SLABS):
            cp = pltpu.make_async_copy(r_hbm.at[:, e, s], g3.at[e, s, pl.ds(1, 2)], ld.at[e, s])
            cp.start()
            loads.append(cp)
    cp = pltpu.make_async_copy(t_hbm, coup, ld.at[0, SLABS])
    cp.start()
    loads.append(cp)

    def stripe(p):
        return pl.ds(pl.multiple_of(p * STRIPE, STRIPE), STRIPE)

    own = pl.ds(2 * me, EN)
    arrays = ((g_hbm, gbuf), (w_hbm, wbuf))

    def local_stripe(a, s):
        return pltpu.make_async_copy(
            arrays[a][0].at[:, :, s, stripe(me)], arrays[a][1].at[s, :, own], fr.at[a, s, 0]
        )

    def forward(a, s, k):
        p = (me + k) % PEERS
        return pltpu.make_async_remote_copy(
            src_ref=arrays[a][0].at[:, :, s, stripe(p)],
            dst_ref=arrays[a][1].at[s, :, own],
            send_sem=fs.at[a, s, k],
            recv_sem=fr.at[a, s, k],
            device_id={"energy": p},
            device_id_type=MESH,
        )

    pl.semaphore_wait(barrier, PEERS - 1 + 2 * (SIDE - 1))
    for s in range(SLABS):
        for k in range(1, PEERS):
            for a in range(2):
                forward(a, s, k).start()
        for a in range(2):
            local_stripe(a, s).start()

    def gather(k, source, target, send, recv, peer):
        return pltpu.make_async_remote_copy(
            src_ref=source, dst_ref=target, send_sem=send, recv_sem=recv,
            device_id=peer, device_id_type=MESH,
        )

    def send_m(e, k, i):
        view = (mh, ml)[i].at[z, e, pl.ds(1, 2)]
        return gather(k, view, view, ms.at[i, e, k], mr.at[i, e, k], z_peer(k))

    def send_n(e, k, i):
        view = (nh, nl)[i].at[x - 1, e]
        return gather(k, view, view, ns.at[i, e, k], nr.at[i, e, k], x_peer(k))

    def upward(act):
        for k in range(1, SIDE):
            pl.when(x + k < SIDE)(lambda k=k: act(k))

    def send_a(e, k):
        view = arow.at[z, e]
        return gather(k, view, view, asend.at[e, k], arecv.at[e, k], z_peer(k))

    def send_r(e, k):
        view = rrow.at[x, e]
        return gather(k, view, view, xs.at[e, k], xr.at[e, k], x_peer(k))

    for cp in loads:
        cp.wait()

    @pl.loop(0, EN)
    def _(e):
        @pl.loop(0, SLABS)
        def _(s):
            g3[e, s, 0] = -g3[e, s, 2]
            high, low = split(left(g3[e, s], coup[0, s], coup[1, s]))
            put3(kh.at[e, s], high)
            put3(kl.at[e, s], low)

        ph[e, 0] = kh[e, 0]
        pw[e, 0] = kl[e, 0]

        @pl.loop(1, SLABS)
        def _(s):
            value = product(kh[e, s], kl[e, s], rows(ph[e, s - 1, 1:3]), rows(pw[e, s - 1, 1:3]))
            high, low = split(value)
            put3(ph.at[e, s], high)
            put3(pw.at[e, s], low)

        mh[z, e] = ph[e, SLABS - 1]
        ml[z, e] = pw[e, SLABS - 1]
        for i in range(2):
            for k in range(1, SIDE):
                send_m(e, k, i).start()

    def convolve(s):
        for a in range(2):
            local_stripe(a, s).wait()
        for k in range(1, PEERS):
            for a in range(2):
                forward(a, s, k).wait_recv()

        @pl.loop(0, STRIPE // 16)
        def _(tr):
            @pl.loop(0, NORB // 128)
            def _(tc):
                rr_ = pl.ds(pl.multiple_of(tr * 16, 16), 16)
                cc_ = pl.ds(pl.multiple_of(tc * 128, 128), 128)
                for part in range(2):
                    for m in range(POINTS):
                        gf[part, m] = gbuf[s, part, m, rr_, cc_].astype(F32)
                        wf[part, m] = wbuf[s, part, m, rr_, cc_].astype(F32)
                for n in range(POINTS):
                    re = None
                    im = None
                    for m in range(max(0, n + MIDDLE + 1 - POINTS), min(POINTS, n + MIDDLE + 1)):
                        l = n - m + MIDDLE
                        a, b = gf[0, m], gf[1, m]
                        c, d = wf[0, l], wf[1, l]
                        r = a * c - b * d
                        i = a * d + b * c
                        re = r if re is None else re + r
                        im = i if im is None else im + i
                    sig[s, 0, n, rr_, cc_] = (im * (-1.0 / POINTS)).astype(BF16)
                    sig[s, 1, n, rr_, cc_] = (re * (1.0 / POINTS)).astype(BF16)

    def giveback(e, s, k):
        p = (me + k) % PEERS
        return pltpu.make_async_remote_copy(
            src_ref=sig.at[s, :, 2 * p + e],
            dst_ref=smat.at[e, s, :, stripe(me)],
            send_sem=rs.at[e, s, k],
            recv_sem=rr.at[e, s, k],
            device_id={"energy": p},
            device_id_type=MESH,
        )

    def keep(e, s):
        return pltpu.make_async_copy(
            sig.at[s, :, 2 * me + e], smat.at[e, s, :, stripe(me)], rr.at[e, s, 0]
        )

    def send_back(e, s):
        for k in range(1, PEERS):
            giveback(e, s, k).start()

    def row_products(e):
        for i in range(2):
            for k in range(1, SIDE):
                send_m(e, k, i).wait_recv()
        eye = (
            lax.broadcasted_iota(jnp.int32, (NORB, NORB), 0)
            == lax.broadcasted_iota(jnp.int32, (NORB, NORB), 1)
        )
        zh[0, 0] = jnp.zeros((NORB, NORB), BF16)
        zh[0, 1] = jnp.where(eye, 1.0, 0.0).astype(BF16)
        zh[0, 2] = jnp.zeros((NORB, NORB), BF16)
        zl[0] = jnp.zeros((3, NORB, NORB), BF16)

        @pl.loop(0, SIDE)
        def _(j):
            now = j % 2

            @pl.when(j == z)
            def _():
                first = jnp.maximum(x - 1, 0)
                vh[e, first] = zh[now]
                vl[e, first] = zl[now]

            mh[j, e, 0] = -mh[j, e, 2]
            ml[j, e, 0] = -ml[j, e, 2]
            value = product(mh[j, e], ml[j, e], rows(zh[now, 1:3]), rows(zl[now, 1:3]))
            high, low = split(value)
            put3(zh.at[1 - now], high)
            put3(zl.at[1 - now], low)

        @pl.when((x > 0) & (x < SIDE - 1))
        def _():
            nh[x - 1, e] = zh[0, 1:3]
            nl[x - 1, e] = zl[0, 1:3]
            for i in range(2):
                upward(lambda k: send_n(e, k, i).start())

        @pl.when(x < SIDE - 1)
        def _():
            wh[e, SIDE - 2] = mh[SIDE - 1, e]
            wl[e, SIDE - 2] = ml[SIDE - 1, e]

            @pl.loop(1, SIDE - 1)
            def _(i):
                j = SIDE - 2 - i
                value = product(
                    wh[e, j + 1], wl[e, j + 1], rows(mh[j + 1, e, 1:3]), rows(ml[j + 1, e, 1:3])
                )
                high, low = split(value)
                put3(wh.at[e, j], high)
                put3(wl.at[e, j], low)

    @pl.loop(0, SLABS - 2)
    def _(s):
        convolve(s)
        send_back(0, s)
        for e in range(EN):
            keep(e, s).start()

    row_products(0)

    @pl.loop(SLABS - 2, SLABS)
    def _(s):
        convolve(s)
        send_back(0, s)
        for e in range(EN):
            keep(e, s).start()

    @pl.loop(0, SLABS)
    def _(s):
        send_back(1, s)

    row_products(1)

    def row_windows(e):
        @pl.loop(1, x)
        def _(i):
            j = x - i
            for part in range(2):
                pltpu.make_async_copy(
                    (nh, nl)[part].at[j - 1, e], (nh, nl)[part].at[j - 1, e], nr.at[part, e, x - j]
                ).wait()
            value = product(vh[e, j], vl[e, j], rows(nh[j - 1, e]), rows(nl[j - 1, e]))
            high, low = split(value)
            put3(vh.at[e, j - 1], high)
            put3(vl.at[e, j - 1], low)

    row_windows(0)

    @pl.loop(0, EN)
    def _(e):
        @pl.loop(0, SLABS)
        def _(s):
            keep(e, s).wait()
            for k in range(1, PEERS):
                giveback(e, s, k).wait_recv()
            mixed = left(g3[e, s], smat[e, s, 0], smat[e, s, 1]).astype(BF16)
            put3(ih, mixed)
            bst[e, s] = right(ih, g3[e, s]).reshape(2, NORB, NORB)

            @pl.when(s > 0)
            def _():
                value = congruence(kh[e, s], kl[e, s], rows(bst[e, s - 1]), ih, il)
                bst[e, s] += value.reshape(2, NORB, NORB)

        arow[z, e] = bst[e, SLABS - 1].astype(BF16)
        for k in (2, 1, 3):
            send_a(e, k).start()

    @pl.loop(0, EN)
    def _(e):
        @pl.when(e == 1)
        def _():
            row_windows(1)

        pre[SIDE] = jnp.zeros((2, NORB, NORB), F32)

        @pl.loop(0, SIDE)
        def _(t):
            k = jnp.where(t < 2, t, SIDE + 1 - t)
            j = (z - k + SIDE) % SIDE

            @pl.when(k > 0)
            def _():
                send_a(e, k).wait_recv()

            @pl.when((x < SIDE - 1) & (j < SIDE - 1))
            def _():
                value = congruence(wh[e, j], wl[e, j], rows(arow[j, e]), ih, il, True)
                pre[SIDE] += value.reshape(2, NORB, NORB)

            @pl.when(j == SIDE - 1)
            def _():
                pre[SIDE] += arow[j, e].astype(F32)

        @pl.when(x < SIDE - 1)
        def _():
            rrow[x, e] = pre[SIDE].astype(BF16)
            for k in range(SIDE - 1, 0, -1):

                @pl.when(x + k < SIDE)
                def _(k=k):
                    send_r(e, k).start()

        pre[0] = jnp.zeros((2, NORB, NORB), F32)
        pre[1] = arow[0, e].astype(F32)

        @pl.when(z > 1)
        def _():
            value = congruence(mh[1, e], ml[1, e], rows(arow[0, e]), ih, il, True)
            pre[2] = value.reshape(2, NORB, NORB) + arow[1, e].astype(F32)

        @pl.when(z > 2)
        def _():
            value = congruence(mh[2, e], ml[2, e], rows(pre[2]), ih, il)
            pre[3] = value.reshape(2, NORB, NORB) + arow[2, e].astype(F32)

        cin[e] = pre[z]

    def store(e, s):
        return pltpu.make_async_copy(bst.at[e, s], out_hbm.at[:, e, s], od.at[e, s])

    @pl.loop(0, EN)
    def _(e):
        @pl.loop(0, x)
        def _(t):
            k = jnp.where(x < SIDE - 1, t + 1, jnp.where(t == 0, SIDE - 1, t))
            j = x - k
            send_r(e, k).wait_recv()
            value = congruence(vh[e, j], vl[e, j], rows(rrow[j, e]), ih, il, True, True)
            cin[e] += value.reshape(2, NORB, NORB)

        @pl.loop(0, SLABS)
        def _(s):
            @pl.when(slab == 0)
            def _():
                bst[e, s] = bst[e, s] * 0.5

            @pl.when(slab > 0)
            def _():
                value = congruence(ph[e, s], pw[e, s], rows(cin[e]), ih, il, True, True)
                bst[e, s] = (bst[e, s] + value.reshape(2, NORB, NORB)) * 0.5

            store(e, s).start()

    for e in range(EN):
        for s in range(SLABS):
            store(e, s).wait()
        for k in range(1, SIDE):
            send_m(e, k, 0).wait_send()
            send_m(e, k, 1).wait_send()
            send_a(e, k).wait_send()
        upward(lambda k: send_r(e, k).wait_send())

        @pl.when((x > 0) & (x < SIDE - 1))
        def _(e=e):
            for i in range(2):
                upward(lambda k: send_n(e, k, i).wait_send())

        for s in range(SLABS):
            for k in range(1, PEERS):
                giveback(e, s, k).wait_send()
    for s in range(SLABS):
        for k in range(1, PEERS):
            for a in range(2):
                forward(a, s, k).wait_send()


def per_device(green_lesser, screened_lesser, green_retarded, coupling):
    block = (NORB, NORB)
    dma = pltpu.SemaphoreType.DMA
    half = pl.pallas_call(
        kernel,
        out_shape=jax.ShapeDtypeStruct((2, EN, SLABS) + block, F32),
        in_specs=[pl.BlockSpec(memory_space=pl.ANY)] * 4,
        out_specs=pl.BlockSpec(memory_space=pl.ANY),
        scratch_shapes=[
            pltpu.VMEM((SLABS, 2, POINTS, STRIPE, NORB), BF16),
            pltpu.VMEM((SLABS, 2, POINTS, STRIPE, NORB), BF16),
            pltpu.VMEM((SLABS, 2, POINTS, STRIPE, NORB), BF16),
            pltpu.VMEM((EN, SLABS, 2) + block, BF16),
            pltpu.VMEM((EN, SLABS, 3) + block, BF16),
            pltpu.VMEM((2, SLABS) + block, BF16),
            pltpu.VMEM((EN, SLABS, 3) + block, BF16),
            pltpu.VMEM((EN, SLABS, 3) + block, BF16),
            pltpu.VMEM((EN, SLABS, 3) + block, BF16),
            pltpu.VMEM((EN, SLABS, 3) + block, BF16),
            pltpu.VMEM((EN, SIDE - 1, 3) + block, BF16),
            pltpu.VMEM((EN, SIDE - 1, 3) + block, BF16),
            pltpu.VMEM((EN, SIDE - 1, 3) + block, BF16),
            pltpu.VMEM((EN, SIDE - 1, 3) + block, BF16),
            pltpu.VMEM((EN, SLABS, 2) + block, F32),
            pltpu.VMEM((EN, 2) + block, F32),
            pltpu.VMEM((SIDE, EN, 3) + block, BF16),
            pltpu.VMEM((SIDE, EN, 3) + block, BF16),
            pltpu.VMEM((SIDE - 2, EN, 2) + block, BF16),
            pltpu.VMEM((SIDE - 2, EN, 2) + block, BF16),
            pltpu.VMEM((SIDE, EN, 2) + block, BF16),
            pltpu.VMEM((SIDE, EN, 2) + block, BF16),
            pltpu.VMEM((2, 3) + block, BF16),
            pltpu.VMEM((2, 3) + block, BF16),
            pltpu.VMEM((SIDE + 1, 2) + block, F32),
            pltpu.VMEM((3,) + block, BF16),
            pltpu.VMEM((3,) + block, BF16),
            pltpu.VMEM((2, POINTS, 16, 128), F32),
            pltpu.VMEM((2, POINTS, 16, 128), F32),
            dma((2, SLABS, PEERS)),
            dma((2, SLABS, PEERS)),
            dma((EN, SLABS, PEERS)),
            dma((EN, SLABS, PEERS)),
            dma((2, EN, SIDE)),
            dma((2, EN, SIDE)),
            dma((2, EN, SIDE)),
            dma((2, EN, SIDE)),
            dma((EN, SIDE)),
            dma((EN, SIDE)),
            dma((EN, SIDE)),
            dma((EN, SIDE)),
            dma((EN, SLABS + 1)),
            dma((EN, SLABS)),
        ],
        compiler_params=pltpu.CompilerParams(
            collective_id=0, has_side_effects=True, vmem_limit_bytes=63000 * 1024
        ),
        name="born_step",
    )(green_lesser, screened_lesser, green_retarded, coupling)
    return half * 2.0


def solution(mesh):
    placed = (
        P(None, "energy", "slab", None, None),
        P(None, "energy", "slab", None, None),
        P(None, "energy", "slab", None, None),
        P(None, "slab", None, None),
    )
    return jax.shard_map(
        per_device,
        mesh=mesh,
        in_specs=placed,
        out_specs=P(None, "energy", "slab", None, None),
        check_vma=False,
    )
```

```python
import jax
import jax.numpy as jnp
from jax import lax
from jax.experimental import pallas as pl
from jax.experimental.pallas import tpu as pltpu
from jax.sharding import PartitionSpec as P

F32 = jnp.float32
BF16 = jnp.bfloat16
NORB = 256
POINTS = 16
MIDDLE = POINTS // 2
PEERS = 8
STRIPE = NORB // PEERS
SLABS = 4
EN = 2
SIDE = 4
MESH = pl.DeviceIdType.MESH


def nn(a, b):
    return lax.dot_general(a, b, (((1,), (0,)), ((), ())), preferred_element_type=F32)


def nt(a, b):
    return lax.dot_general(a, b, (((1,), (1,)), ((), ())), preferred_element_type=F32)


def rows(pair):
    return pair.reshape(2 * NORB, NORB)


def left(x3, re, im):
    return nn(rows(x3[1:3]), re) + nn(rows(x3[0:2]), im)


def right(i3, x3):
    return nt(rows(i3[1:3]), x3[1]) + nt(rows(i3[0:2]), x3[0])


def split(value):
    high = value.astype(BF16)
    low = (value - high.astype(F32)).astype(BF16)
    return high, low


def put3(ref, pair):
    ref[1:3] = pair.reshape(2, NORB, NORB)
    ref[0] = -pair[NORB:]


def product(xh, xl, ch, cl):
    total = left(xh, ch[:NORB], ch[NORB:]) + left(xl, ch[:NORB], ch[NORB:])
    if cl is not None:
        total = total + left(xh, cl[:NORB], cl[NORB:])
    return total


def congruence(xh, xl, state, ih, il, exact=False, brief=False):
    high, low = (state.astype(BF16), None) if exact else split(state)
    inner = product(xh, xl, high, low)
    if brief:
        put3(ih, inner.astype(BF16))
        return right(ih, xh) + right(ih, xl)
    high, low = split(inner)
    put3(ih, high)
    put3(il, low)
    return right(ih, xh) + right(il, xh) + right(ih, xl)


def kernel(
    g_hbm, w_hbm, r_hbm, t_hbm, out_hbm,
    gbuf, wbuf, sig, smat, g3, coup, kh, kl, ph, pw, vh, vl, wh, wl, bst, cin,
    mh, ml, nh, nl, arow, rrow, zh, zl, pre, ih, il, gf, wf,
    fs, fr, rs, rr, ms, mr, ns, nr, asend, arecv, xs, xr, ld, od,
):
    slab = lax.axis_index("slab")
    me = lax.axis_index("energy")
    x = slab // SIDE
    z = slab % SIDE

    def energy_peer(k):
        return {"energy": (me + k) % PEERS}

    def z_peer(k):
        return {"slab": x * SIDE + (z + k) % SIDE}

    def x_peer(k):
        return {"slab": ((x + k) % SIDE) * SIDE + z}

    barrier = pltpu.get_barrier_semaphore()
    for k in range(1, PEERS):
        pl.semaphore_signal(barrier, inc=1, device_id=energy_peer(k), device_id_type=MESH)
    for k in range(1, SIDE):
        pl.semaphore_signal(barrier, inc=1, device_id=z_peer(k), device_id_type=MESH)
        pl.semaphore_signal(barrier, inc=1, device_id=x_peer(k), device_id_type=MESH)

    loads = []
    for e in range(EN):
        for s in range(SLABS):
            cp = pltpu.make_async_copy(r_hbm.at[:, e, s], g3.at[e, s, pl.ds(1, 2)], ld.at[e, s])
            cp.start()
            loads.append(cp)
    cp = pltpu.make_async_copy(t_hbm, coup, ld.at[0, SLABS])
    cp.start()
    loads.append(cp)

    def stripe(p):
        return pl.ds(pl.multiple_of(p * STRIPE, STRIPE), STRIPE)

    own = pl.ds(2 * me, EN)
    arrays = ((g_hbm, gbuf), (w_hbm, wbuf))

    def local_stripe(a, s):
        return pltpu.make_async_copy(
            arrays[a][0].at[:, :, s, stripe(me)], arrays[a][1].at[s, :, own], fr.at[a, s, 0]
        )

    def forward(a, s, k):
        p = (me + k) % PEERS
        return pltpu.make_async_remote_copy(
            src_ref=arrays[a][0].at[:, :, s, stripe(p)],
            dst_ref=arrays[a][1].at[s, :, own],
            send_sem=fs.at[a, s, k],
            recv_sem=fr.at[a, s, k],
            device_id={"energy": p},
            device_id_type=MESH,
        )

    pl.semaphore_wait(barrier, PEERS - 1 + 2 * (SIDE - 1))
    for s in range(SLABS):
        for k in range(1, PEERS):
            for a in range(2):
                forward(a, s, k).start()
        for a in range(2):
            local_stripe(a, s).start()

    def gather(k, source, target, send, recv, peer):
        return pltpu.make_async_remote_copy(
            src_ref=source, dst_ref=target, send_sem=send, recv_sem=recv,
            device_id=peer, device_id_type=MESH,
        )

    def send_m(e, k, i):
        view = (mh, ml)[i].at[z, e, pl.ds(1, 2)]
        return gather(k, view, view, ms.at[i, e, k], mr.at[i, e, k], z_peer(k))

    def send_n(e, k, i):
        view = (nh, nl)[i].at[x - 1, e]
        return gather(k, view, view, ns.at[i, e, k], nr.at[i, e, k], x_peer(k))

    def upward(act):
        for k in range(1, SIDE):
            pl.when(x + k < SIDE)(lambda k=k: act(k))

    def send_a(e, k):
        view = arow.at[z, e]
        return gather(k, view, view, asend.at[e, k], arecv.at[e, k], z_peer(k))

    def send_r(e, k):
        view = rrow.at[x, e]
        return gather(k, view, view, xs.at[e, k], xr.at[e, k], x_peer(k))

    for cp in loads:
        cp.wait()

    @pl.loop(0, EN)
    def _(e):
        @pl.loop(0, SLABS)
        def _(s):
            g3[e, s, 0] = -g3[e, s, 2]
            high, low = split(left(g3[e, s], coup[0, s], coup[1, s]))
            put3(kh.at[e, s], high)
            put3(kl.at[e, s], low)

        ph[e, 0] = kh[e, 0]
        pw[e, 0] = kl[e, 0]

        @pl.loop(1, SLABS)
        def _(s):
            value = product(kh[e, s], kl[e, s], rows(ph[e, s - 1, 1:3]), rows(pw[e, s - 1, 1:3]))
            high, low = split(value)
            put3(ph.at[e, s], high)
            put3(pw.at[e, s], low)

        mh[z, e] = ph[e, SLABS - 1]
        ml[z, e] = pw[e, SLABS - 1]
        for i in range(2):
            for k in range(1, SIDE):
                send_m(e, k, i).start()

    def convolve(s):
        for a in range(2):
            local_stripe(a, s).wait()
        for k in range(1, PEERS):
            for a in range(2):
                forward(a, s, k).wait_recv()

        @pl.loop(0, STRIPE // 16)
        def _(tr):
            @pl.loop(0, NORB // 128)
            def _(tc):
                rr_ = pl.ds(pl.multiple_of(tr * 16, 16), 16)
                cc_ = pl.ds(pl.multiple_of(tc * 128, 128), 128)
                for part in range(2):
                    for m in range(POINTS):
                        gf[part, m] = gbuf[s, part, m, rr_, cc_].astype(F32)
                        wf[part, m] = wbuf[s, part, m, rr_, cc_].astype(F32)
                for n in range(POINTS):
                    re = None
                    im = None
                    for m in range(max(0, n + MIDDLE + 1 - POINTS), min(POINTS, n + MIDDLE + 1)):
                        l = n - m + MIDDLE
                        a, b = gf[0, m], gf[1, m]
                        c, d = wf[0, l], wf[1, l]
                        r = a * c - b * d
                        i = a * d + b * c
                        re = r if re is None else re + r
                        im = i if im is None else im + i
                    sig[s, 0, n, rr_, cc_] = (im * (-1.0 / POINTS)).astype(BF16)
                    sig[s, 1, n, rr_, cc_] = (re * (1.0 / POINTS)).astype(BF16)

    def giveback(e, s, k):
        p = (me + k) % PEERS
        return pltpu.make_async_remote_copy(
            src_ref=sig.at[s, :, 2 * p + e],
            dst_ref=smat.at[e, s, :, stripe(me)],
            send_sem=rs.at[e, s, k],
            recv_sem=rr.at[e, s, k],
            device_id={"energy": p},
            device_id_type=MESH,
        )

    def keep(e, s):
        return pltpu.make_async_copy(
            sig.at[s, :, 2 * me + e], smat.at[e, s, :, stripe(me)], rr.at[e, s, 0]
        )

    def send_back(e, s):
        for k in range(1, PEERS):
            giveback(e, s, k).start()

    def row_products(e):
        for i in range(2):
            for k in range(1, SIDE):
                send_m(e, k, i).wait_recv()
        eye = (
            lax.broadcasted_iota(jnp.int32, (NORB, NORB), 0)
            == lax.broadcasted_iota(jnp.int32, (NORB, NORB), 1)
        )
        zh[0, 0] = jnp.zeros((NORB, NORB), BF16)
        zh[0, 1] = jnp.where(eye, 1.0, 0.0).astype(BF16)
        zh[0, 2] = jnp.zeros((NORB, NORB), BF16)
        zl[0] = jnp.zeros((3, NORB, NORB), BF16)

        @pl.loop(0, SIDE)
        def _(j):
            now = j % 2

            @pl.when(j == z)
            def _():
                first = jnp.maximum(x - 1, 0)
                vh[e, first] = zh[now]
                vl[e, first] = zl[now]

            mh[j, e, 0] = -mh[j, e, 2]
            ml[j, e, 0] = -ml[j, e, 2]
            value = product(mh[j, e], ml[j, e], rows(zh[now, 1:3]), rows(zl[now, 1:3]))
            high, low = split(value)
            put3(zh.at[1 - now], high)
            put3(zl.at[1 - now], low)

        @pl.when((x > 0) & (x < SIDE - 1))
        def _():
            nh[x - 1, e] = zh[0, 1:3]
            nl[x - 1, e] = zl[0, 1:3]
            for i in range(2):
                upward(lambda k: send_n(e, k, i).start())

        @pl.when(x < SIDE - 1)
        def _():
            wh[e, SIDE - 2] = mh[SIDE - 1, e]
            wl[e, SIDE - 2] = ml[SIDE - 1, e]

            @pl.loop(1, SIDE - 1)
            def _(i):
                j = SIDE - 2 - i
                value = product(
                    wh[e, j + 1], wl[e, j + 1], rows(mh[j + 1, e, 1:3]), rows(ml[j + 1, e, 1:3])
                )
                high, low = split(value)
                put3(wh.at[e, j], high)
                put3(wl.at[e, j], low)

    @pl.loop(0, SLABS - 2)
    def _(s):
        convolve(s)
        send_back(0, s)
        for e in range(EN):
            keep(e, s).start()

    row_products(0)

    @pl.loop(SLABS - 2, SLABS)
    def _(s):
        convolve(s)
        send_back(0, s)
        for e in range(EN):
            keep(e, s).start()

    @pl.loop(0, SLABS)
    def _(s):
        send_back(1, s)

    row_products(1)

    def row_windows(e):
        @pl.loop(1, x)
        def _(i):
            j = x - i
            for part in range(2):
                pltpu.make_async_copy(
                    (nh, nl)[part].at[j - 1, e], (nh, nl)[part].at[j - 1, e], nr.at[part, e, x - j]
                ).wait()
            value = product(vh[e, j], vl[e, j], rows(nh[j - 1, e]), rows(nl[j - 1, e]))
            high, low = split(value)
            put3(vh.at[e, j - 1], high)
            put3(vl.at[e, j - 1], low)

    row_windows(0)

    @pl.loop(0, EN)
    def _(e):
        @pl.loop(0, SLABS)
        def _(s):
            keep(e, s).wait()
            for k in range(1, PEERS):
                giveback(e, s, k).wait_recv()
            mixed = left(g3[e, s], smat[e, s, 0], smat[e, s, 1]).astype(BF16)
            put3(ih, mixed)
            bst[e, s] = right(ih, g3[e, s]).reshape(2, NORB, NORB)

            @pl.when(s > 0)
            def _():
                value = congruence(kh[e, s], kl[e, s], rows(bst[e, s - 1]), ih, il)
                bst[e, s] += value.reshape(2, NORB, NORB)

        arow[z, e] = bst[e, SLABS - 1].astype(BF16)
        for k in (1, 3, 2):
            send_a(e, k).start()

    @pl.loop(0, EN)
    def _(e):
        @pl.when(e == 1)
        def _():
            row_windows(1)

        pre[SIDE] = jnp.zeros((2, NORB, NORB), F32)

        @pl.loop(0, SIDE)
        def _(t):
            k = jnp.where(t < 2, t, SIDE + 1 - t)
            j = (z - k + SIDE) % SIDE

            @pl.when(k > 0)
            def _():
                send_a(e, k).wait_recv()

            @pl.when((x < SIDE - 1) & (j < SIDE - 1))
            def _():
                value = congruence(wh[e, j], wl[e, j], rows(arow[j, e]), ih, il, True)
                pre[SIDE] += value.reshape(2, NORB, NORB)

            @pl.when(j == SIDE - 1)
            def _():
                pre[SIDE] += arow[j, e].astype(F32)

        @pl.when(x < SIDE - 1)
        def _():
            rrow[x, e] = pre[SIDE].astype(BF16)
            for k in range(SIDE - 1, 0, -1):

                @pl.when(x + k < SIDE)
                def _(k=k):
                    send_r(e, k).start()

        pre[0] = jnp.zeros((2, NORB, NORB), F32)
        pre[1] = arow[0, e].astype(F32)

        @pl.when(z > 1)
        def _():
            value = congruence(mh[1, e], ml[1, e], rows(arow[0, e]), ih, il, True)
            pre[2] = value.reshape(2, NORB, NORB) + arow[1, e].astype(F32)

        @pl.when(z > 2)
        def _():
            value = congruence(mh[2, e], ml[2, e], rows(pre[2]), ih, il)
            pre[3] = value.reshape(2, NORB, NORB) + arow[2, e].astype(F32)

        cin[e] = pre[z]

    def store(e, s):
        return pltpu.make_async_copy(bst.at[e, s], out_hbm.at[:, e, s], od.at[e, s])

    @pl.loop(0, EN)
    def _(e):
        @pl.loop(0, x)
        def _(t):
            k = jnp.where(x < SIDE - 1, t + 1, jnp.where(t == 0, SIDE - 1, t))
            j = x - k
            send_r(e, k).wait_recv()
            value = congruence(vh[e, j], vl[e, j], rows(rrow[j, e]), ih, il, True)
            cin[e] += value.reshape(2, NORB, NORB)

        @pl.loop(0, SLABS)
        def _(s):
            @pl.when(slab == 0)
            def _():
                bst[e, s] = bst[e, s] * 0.5

            @pl.when(slab > 0)
            def _():
                value = congruence(ph[e, s], pw[e, s], rows(cin[e]), ih, il, True, True)
                bst[e, s] = (bst[e, s] + value.reshape(2, NORB, NORB)) * 0.5

            store(e, s).start()

    for e in range(EN):
        for s in range(SLABS):
            store(e, s).wait()
        for k in range(1, SIDE):
            send_m(e, k, 0).wait_send()
            send_m(e, k, 1).wait_send()
            send_a(e, k).wait_send()
        upward(lambda k: send_r(e, k).wait_send())

        @pl.when((x > 0) & (x < SIDE - 1))
        def _(e=e):
            for i in range(2):
                upward(lambda k: send_n(e, k, i).wait_send())

        for s in range(SLABS):
            for k in range(1, PEERS):
                giveback(e, s, k).wait_send()
    for s in range(SLABS):
        for k in range(1, PEERS):
            for a in range(2):
                forward(a, s, k).wait_send()


def per_device(green_lesser, screened_lesser, green_retarded, coupling):
    block = (NORB, NORB)
    dma = pltpu.SemaphoreType.DMA
    half = pl.pallas_call(
        kernel,
        out_shape=jax.ShapeDtypeStruct((2, EN, SLABS) + block, F32),
        in_specs=[pl.BlockSpec(memory_space=pl.ANY)] * 4,
        out_specs=pl.BlockSpec(memory_space=pl.ANY),
        scratch_shapes=[
            pltpu.VMEM((SLABS, 2, POINTS, STRIPE, NORB), BF16),
            pltpu.VMEM((SLABS, 2, POINTS, STRIPE, NORB), BF16),
            pltpu.VMEM((SLABS, 2, POINTS, STRIPE, NORB), BF16),
            pltpu.VMEM((EN, SLABS, 2) + block, BF16),
            pltpu.VMEM((EN, SLABS, 3) + block, BF16),
            pltpu.VMEM((2, SLABS) + block, BF16),
            pltpu.VMEM((EN, SLABS, 3) + block, BF16),
            pltpu.VMEM((EN, SLABS, 3) + block, BF16),
            pltpu.VMEM((EN, SLABS, 3) + block, BF16),
            pltpu.VMEM((EN, SLABS, 3) + block, BF16),
            pltpu.VMEM((EN, SIDE - 1, 3) + block, BF16),
            pltpu.VMEM((EN, SIDE - 1, 3) + block, BF16),
            pltpu.VMEM((EN, SIDE - 1, 3) + block, BF16),
            pltpu.VMEM((EN, SIDE - 1, 3) + block, BF16),
            pltpu.VMEM((EN, SLABS, 2) + block, F32),
            pltpu.VMEM((EN, 2) + block, F32),
            pltpu.VMEM((SIDE, EN, 3) + block, BF16),
            pltpu.VMEM((SIDE, EN, 3) + block, BF16),
            pltpu.VMEM((SIDE - 2, EN, 2) + block, BF16),
            pltpu.VMEM((SIDE - 2, EN, 2) + block, BF16),
            pltpu.VMEM((SIDE, EN, 2) + block, BF16),
            pltpu.VMEM((SIDE, EN, 2) + block, BF16),
            pltpu.VMEM((2, 3) + block, BF16),
            pltpu.VMEM((2, 3) + block, BF16),
            pltpu.VMEM((SIDE + 1, 2) + block, F32),
            pltpu.VMEM((3,) + block, BF16),
            pltpu.VMEM((3,) + block, BF16),
            pltpu.VMEM((2, POINTS, 16, 128), F32),
            pltpu.VMEM((2, POINTS, 16, 128), F32),
            dma((2, SLABS, PEERS)),
            dma((2, SLABS, PEERS)),
            dma((EN, SLABS, PEERS)),
            dma((EN, SLABS, PEERS)),
            dma((2, EN, SIDE)),
            dma((2, EN, SIDE)),
            dma((2, EN, SIDE)),
            dma((2, EN, SIDE)),
            dma((EN, SIDE)),
            dma((EN, SIDE)),
            dma((EN, SIDE)),
            dma((EN, SIDE)),
            dma((EN, SLABS + 1)),
            dma((EN, SLABS)),
        ],
        compiler_params=pltpu.CompilerParams(
            collective_id=0, has_side_effects=True, vmem_limit_bytes=63000 * 1024
        ),
        name="born_step",
    )(green_lesser, screened_lesser, green_retarded, coupling)
    return half * 2.0


def solution(mesh):
    placed = (
        P(None, "energy", "slab", None, None),
        P(None, "energy", "slab", None, None),
        P(None, "energy", "slab", None, None),
        P(None, "slab", None, None),
    )
    return jax.shard_map(
        per_device,
        mesh=mesh,
        in_specs=placed,
        out_specs=P(None, "energy", "slab", None, None),
        check_vma=False,
    )
```
